512 devices in a mesh: seq: 64 (over y, x, z_hi), head: 8 (over z_lo, core).
Axes of the slice: x: 4, y: 4, z: 16 (z_hi: 4, z_lo: 4; z = z_hi * 4 + z_lo), core: 2. Of those that a mesh axis runs over, the one named last changes fastest.
Arguments:
- inputs: bfloat16 [32768, 4096], P('seq', 'head'), may hold values from -6 to 6
- latent: float32 [4096, 2048], P('seq', 'head'), as said below
- queries: bfloat16 [32768, 2048], P('seq', 'head'), may hold values from -6 to 6
- keys: bfloat16 [32768, 2048], P('seq', 'head'), may hold values from -6 to 6
- grad_out: bfloat16 [32768, 2048], P('seq', 'head'), may hold values from -6 to 6
Outputs:
- attn_out: bfloat16 [32768, 2048], P('seq', 'head')
- grad_queries: bfloat16 [32768, 2048], P('seq', 'head')
- grad_keys: bfloat16 [32768, 2048], P('seq', 'head')
- grad_latent: float32 [4096, 2048], P('seq', 'head')
The draws below stay inside these ranges and needn't reach their ends.
Inputs may be any that keep to these rules, and one draw needn't show every extreme that they name: `latent`: no entry's magnitude lies between 0.67 and 1.5 times half of its column's mean magnitude.
All inputs are finite; a program needn't handle non-finite values.
Results may differ from the reference program's by a relative error of at most 0.014.
Values may be sent and summed in bfloat16 or wider, within the bound.
A program may use at most 64 MiB of HBM per device.

```python
import math
import jax
import jax.numpy as jnp
from jax import lax

D = 4096
DK = 128
BLOCK = 128
HEADS = 16
TOKENS = 32768


def draw_latent(key, part):
    mixed_key = jax.random.fold_in(key, 11)
    key_band, key_small, key_large, key_sign, key_column = jax.random.split(mixed_key, 5)
    grid_shape = (D, HEADS * DK)
    share = 1.0 / 3.0
    banded = jax.random.uniform(key_band, grid_shape) < share
    small_size = jax.random.uniform(key_small, grid_shape, minval=0.02, maxval=0.2)
    large_size = jax.random.uniform(key_large, grid_shape, minval=0.7, maxval=1.5)
    ternary_signs = jnp.where(jax.random.bernoulli(key_sign, 0.5, grid_shape), 1.0, -1.0)
    column_base = jnp.exp(jax.random.uniform(key_column, (1, HEADS * DK), minval=math.log(0.5), maxval=math.log(2.0))) / math.sqrt(D)
    return (ternary_signs * jnp.where(banded, small_size, large_size) * column_base).astype(jnp.float32)


def level_of(own_key, shape, pieces, least, top_value):
    def one(axis_at, shards_of):
        heights = jax.random.uniform(jax.random.fold_in(jax.random.fold_in(own_key, 6), axis_at), (shards_of,), jnp.float32, least / len(pieces), top_value / len(pieces))
        return jnp.repeat(jnp.exp(heights), shape[axis_at] // shards_of).reshape((-1,) + (1,) * (len(shape) - axis_at - 1))

    level = one(*pieces[0])
    for cut in pieces[1:]:
        level = level * one(*cut)
    return level


def normal_values(stream_key, shape, spread, limit, pieces=(), dtype=jnp.bfloat16):
    result = spread * jax.random.normal(stream_key, shape, jnp.float32)
    if pieces:
        result = result * level_of(stream_key, shape, pieces, -0.22, 0.18)
    return jnp.clip(result, -limit, limit).astype(dtype)


def setup_inputs(seed: int = 0) -> dict:
    key_of = jax.random.split(jax.random.key(seed), 6)
    inputs = normal_values(key_of[0], (TOKENS, D), 1.0, 6.0, ((0, 64), (1, 8)))
    latent = draw_latent(jax.random.fold_in(key_of[5], 71), 0)
    queries = normal_values(key_of[2], (TOKENS, HEADS * DK), 1.0, 6.0, ((0, 64), (1, 8)))
    keys = normal_values(key_of[3], (TOKENS, HEADS * DK), 1.0, 6.0, ((0, 64), (1, 8)))
    grad_out = normal_values(key_of[4], (TOKENS, HEADS * DK), 1.0, 6.0, ((0, 64), (1, 8)))
    return dict(inputs=inputs, latent=latent, queries=queries, keys=keys, grad_out=grad_out)


absmean_eps = 1e-05
norm_eps = 1e-06

def ternarize(weights, column_scale):
    halfway = 0.5 * column_scale
    ternary_signs = jnp.where(weights > halfway, 1.0, jnp.where(weights < -halfway, -1.0, 0.0))
    return (ternary_signs * column_scale).astype(jnp.bfloat16)

def blocked(matrix):
    return matrix.reshape(TOKENS // BLOCK, BLOCK, HEADS, DK).astype(jnp.float32)

def rounded(matrix):
    return lax.optimization_barrier(matrix.astype(jnp.bfloat16)).astype(jnp.float32)

def reference(inputs, latent, queries, keys, grad_out):
    highest = lax.Precision.HIGHEST
    column_scale = lax.optimization_barrier(jnp.mean(jnp.abs(latent), axis=0)) + absmean_eps
    weights = ternarize(latent, column_scale)
    values_flat = jnp.dot(inputs, weights, preferred_element_type=jnp.float32)
    query_blocks = blocked(queries)
    key_blocks = blocked(keys)
    value_blocks = rounded(blocked(values_flat))
    causal = jnp.tril(jnp.ones((BLOCK, BLOCK), jnp.bool_))
    scores = rounded(jnp.where(causal, jnp.einsum('bthd,bshd->bhts', query_blocks, key_blocks, precision=highest), 0.0))
    within = jnp.einsum('bhts,bshd->bthd', scores, value_blocks, precision=highest)
    block_states = jnp.einsum('bshd,bshe->bhde', key_blocks, value_blocks, precision=highest)
    prior = jnp.cumsum(block_states, axis=0) - block_states
    across = jnp.einsum('bthd,bhde->bthe', query_blocks, prior, precision=highest)
    mixed = within + across
    root_mean = jnp.sqrt(lax.optimization_barrier(jnp.mean(mixed * mixed, axis=-1, keepdims=True)) + norm_eps)
    normed = mixed / root_mean
    attn_out = normed.astype(jnp.bfloat16).reshape(TOKENS, HEADS * DK)
    upstream = blocked(grad_out)
    inner_mean = lax.optimization_barrier(jnp.mean(upstream * normed, axis=-1, keepdims=True))
    grad_mixed = rounded((upstream - normed * inner_mean) / root_mean)
    grad_states = jnp.einsum('bthd,bthe->bhde', query_blocks, grad_mixed, precision=highest)
    following = lax.optimization_barrier(jnp.sum(grad_states, axis=0))[None] - jnp.cumsum(grad_states, axis=0)
    grad_scores = rounded(jnp.where(causal, jnp.einsum('bthe,bshe->bhts', grad_mixed, value_blocks, precision=highest), 0.0))
    grad_query = jnp.einsum('bhts,bshd->bthd', grad_scores, key_blocks, precision=highest) + jnp.einsum('bthe,bhde->bthd', grad_mixed, prior, precision=highest)
    grad_key = jnp.einsum('bhts,bthd->bshd', grad_scores, query_blocks, precision=highest) + jnp.einsum('bshe,bhde->bshd', value_blocks, following, precision=highest)
    grad_value = jnp.einsum('bhts,bthe->bshe', scores, grad_mixed, precision=highest) + jnp.einsum('bshd,bhde->bshe', key_blocks, following, precision=highest)
    grad_flat = grad_value.astype(jnp.bfloat16).reshape(TOKENS, HEADS * DK)
    grad_latent = lax.dot_general(inputs, grad_flat, (((0,), (0,)), ((), ())), preferred_element_type=jnp.float32)
    grad_queries = grad_query.astype(jnp.bfloat16).reshape(TOKENS, HEADS * DK)
    grad_keys = grad_key.astype(jnp.bfloat16).reshape(TOKENS, HEADS * DK)
    return (attn_out, grad_queries, grad_keys, grad_latent)
```

```python
import functools

import jax
import jax.numpy as jnp
from jax import lax
from jax.experimental import pallas as pl
from jax.experimental.pallas import tpu as pltpu
from jax.sharding import Mesh
from jax.sharding import PartitionSpec as P

DK = 128
BLOCK = 128
HEAD = ("head_0", "head_1")
SEQ = ("seq_0", "seq_1", "seq_2")
ID = pl.DeviceIdType.MESH
CHUNKS = 4

absmean_eps = 1e-05
norm_eps = 1e-06

f32 = jnp.float32
bf16 = jnp.bfloat16


def dot(a, b, contract):
    return lax.dot_general(a, b, ((contract[:1], contract[1:]), ((), ())), preferred_element_type=f32)


NN, NT, TN = (1, 0), (1, 1), (0, 0)


def exchange(axis, count, source, target, send, recv):
    position = lax.axis_index(axis)
    copies = []
    for kk in range(1, count):
        peer = lax.rem(position + kk, count)
        copy = pltpu.make_async_remote_copy(
            src_ref=source(peer),
            dst_ref=target(kk),
            send_sem=send.at[kk - 1],
            recv_sem=recv.at[kk - 1],
            device_id={axis: peer},
            device_id_type=ID,
        )
        copy.start()
        copies.append(copy)
    return copies


def arrive(copies):
    for copy in copies:
        copy.wait_recv()


def kernel(
    sizes, x_ref, latent_ref, q_ref, k_ref, go_ref, attn_ref, gq_ref, gk_ref, gl_ref,
    wa, wb, wt, xg, acc, v, sc, st, prior, within, gm, gs, gkp, gvp, gvt, loc, scan_send, scan_recv, inc,
    pa, pb, ra1, rb1, sa2, sb2, ra2, rb2, tz, tzf, rz,
    own_sem, wz_s, wz_r, w2_s, w2_r, w3_s, w3_r, xp_s, xm_s, xs_s, xl_r, xs_r, scan_s, scan_r, g_s, g_r,
):
    ny, nx, nz, nl = sizes
    yy, xx, zh = (lax.axis_index(a) for a in SEQ)
    zl, cc = (lax.axis_index(a) for a in HEAD)
    tokens, feats = x_ref.shape
    rows, columns = latent_ref.shape
    half = rows // 2
    heads = columns // DK
    blocks = tokens // BLOCK
    step = tokens // CHUNKS
    sent = []

    own_x = pltpu.make_async_copy(x_ref, xg.at[zl, cc], own_sem)
    own_x.start()
    at_a = (yy * nx + xx) * nz
    at_b = (xx * ny + yy) * nz
    latent16 = latent_ref[...].astype(bf16)
    wa[at_a + zh] = latent16[:half]
    wb[at_b + zh] = latent16[half:]

    barrier = pltpu.get_barrier_semaphore()
    for axis, count in (("seq_2", nz), ("seq_1", nx), ("seq_0", ny), ("head_1", 2)):
        position = lax.axis_index(axis)
        for kk in range(1, count):
            pl.semaphore_signal(
                barrier, inc=1, device_id={axis: lax.rem(position + kk, count)}, device_id_type=ID
            )

    @pl.when(zl > 0)
    def _():
        pl.semaphore_signal(barrier, inc=1, device_id={"head_0": zl - 1}, device_id_type=ID)

    @pl.when(zl < nl - 1)
    def _():
        pl.semaphore_signal(barrier, inc=1, device_id={"head_0": zl + 1}, device_id_type=ID)

    partners = (nz - 1) + (nx - 1) + (ny - 1) + 1
    neighbours = jnp.where(zl > 0, 1, 0) + jnp.where(zl < nl - 1, 1, 0)
    pl.semaphore_wait(barrier, partners + neighbours)

    wz = exchange("seq_2", nz, lambda p: wa.at[at_a + zh], lambda kk: wa.at[at_a + zh], wz_s.at[0], wz_r.at[0])
    wz += exchange("seq_2", nz, lambda p: wb.at[at_b + zh], lambda kk: wb.at[at_b + zh], wz_s.at[1], wz_r.at[1])
    sent += wz

    def rows_of(ref, j):
        return ref.at[pl.ds(pl.multiple_of(j * step, step), step)]

    def line_copy(block, j, up, own):
        place = rows_of(xg.at[block, cc], j)
        return pltpu.make_async_remote_copy(
            src_ref=rows_of(x_ref, j) if own else place,
            dst_ref=place,
            send_sem=(xp_s if up else xm_s).at[block, j],
            recv_sem=xl_r.at[block, j],
            device_id={"head_0": zl + 1 if up else zl - 1},
            device_id_type=ID,
        )

    def side_copy(block, j, own):
        place = rows_of(xg.at[block, cc], j)
        return pltpu.make_async_remote_copy(
            src_ref=rows_of(x_ref, j) if own else place,
            dst_ref=place,
            send_sem=xs_s.at[block, j],
            recv_sem=xs_r.at[block, j],
            device_id={"head_1": 1 - cc},
            device_id_type=ID,
        )

    @pl.loop(0, CHUNKS)
    def _(j):
        @pl.when(zl < nl - 1)
        def _():
            line_copy(zl, j, True, True).start()

        @pl.when(zl > 0)
        def _():
            line_copy(zl, j, False, True).start()

    @pl.loop(0, CHUNKS)
    def _(j):
        side_copy(zl, j, True).start()

    def relay(distance):
        @pl.loop(0, CHUNKS)
        def _(j):
            @pl.when(zl >= distance)
            def _():
                block = zl - distance
                line_copy(block, j, True, False).wait_recv()

                @pl.when(zl < nl - 1)
                def _():
                    line_copy(block, j, True, False).start()

                side_copy(block, j, False).start()

            @pl.when(zl + distance < nl)
            def _():
                block = zl + distance
                line_copy(block, j, False, False).wait_recv()

                @pl.when(zl > 0)
                def _():
                    line_copy(block, j, False, False).start()

                side_copy(block, j, False).start()

    causal = lax.broadcasted_iota(jnp.int32, (BLOCK, BLOCK), 0) >= lax.broadcasted_iota(
        jnp.int32, (BLOCK, BLOCK), 1
    )

    def each_block(body):
        @pl.loop(0, blocks)
        def _(b):
            at = pl.ds(pl.multiple_of(b * BLOCK, BLOCK), BLOCK)
            for i in range(heads):
                body(b, i, at, slice(i * DK, (i + 1) * DK))

    def scores_body(b, i, at, cols):
        s = dot(q_ref[at, cols], k_ref[at, cols], NT)
        sc[b, i] = jnp.where(causal, s, 0.0).astype(bf16)

    each_block(scores_body)

    arrive(wz)
    mine_a = wa.at[pl.ds(at_a, nz)]
    mine_b = wb.at[pl.ds(at_b, nz)]
    w2a = exchange("seq_1", nx, lambda p: mine_a, lambda kk: mine_a, w2_s.at[0], w2_r.at[0])
    w2b = exchange("seq_0", ny, lambda p: mine_b, lambda kk: mine_b, w2_s.at[1], w2_r.at[1])
    sent += w2a + w2b
    relay(1)
    row_a = wa.at[pl.ds(yy * nx * nz, nx * nz)]
    row_b = wb.at[pl.ds(xx * ny * nz, ny * nz)]
    arrive(w2a)
    w3a = exchange("seq_0", ny, lambda p: row_a, lambda kk: row_a, w3_s.at[0], w3_r.at[0])
    arrive(w2b)
    w3b = exchange("seq_1", nx, lambda p: row_b, lambda kk: row_b, w3_s.at[1], w3_r.at[1])
    sent += w3a + w3b
    for distance in range(2, nl - 1):
        relay(distance)
    arrive(w3a)
    arrive(w3b)

    def magnitude(s, total):
        both = jnp.abs(wa[s].astype(f32)) + jnp.abs(wb[s].astype(f32))
        return total + both.reshape(half // 8, 8, columns).sum(axis=0)

    total = lax.fori_loop(0, ny * nx * nz, magnitude, jnp.zeros((8, columns), f32))
    scale = total.sum(axis=0, keepdims=True) / (ny * nx * nz * rows) + absmean_eps
    halfway = 0.5 * scale

    def ternary(w):
        w = w.astype(f32)
        return jnp.where(w > halfway, scale, jnp.where(w < -halfway, -scale, 0.0)).astype(bf16)

    @pl.loop(0, ny * nx)
    def _(p):
        other = lax.rem(p, nx) * ny + p // nx
        for z in range(nz):
            at = pl.multiple_of((p * nz + z) * rows, rows)
            wt[pl.ds(at, half)] = ternary(wa[p * nz + z])
            wt[pl.ds(pl.multiple_of(at + half, half), half)] = ternary(wb[other * nz + z])

    relay(nl - 1)
    own_x.wait()

    @pl.loop(0, nl)
    def _(block):
        @pl.loop(0, CHUNKS)
        def _(j):
            side_copy(block, j, False).wait_recv()

    acc[...] = jnp.zeros_like(acc)

    @pl.loop(0, nl * 2)
    def _(h):
        at = pl.ds(pl.multiple_of(h * feats, feats), feats)
        acc[...] += dot(xg[h // 2, lax.rem(h, 2)], wt[at], NN)

    v[...] = acc[...].astype(bf16)

    for i in range(heads):
        loc[i] = jnp.zeros((DK, DK), f32)

    def state_body(b, i, at, cols):
        s = dot(k_ref[at, cols], v[at, cols], TN)
        st[b, i] = s
        loc[i] += s

    each_block(state_body)

    def scan(which, reverse):
        def earlier(p, mine):
            return p > mine if reverse else p < mine

        send, recv = scan_send.at[which], scan_recv.at[which]

        def go(axis, count, i, stage, source):
            slot = i * 3 + stage
            copies = exchange(
                axis, count, source, lambda kk: recv.at[slot, kk - 1],
                scan_s.at[which, slot], scan_r.at[which, slot],
            )
            sent.extend(copies)
            return copies

        def collect(axis, count, i, stage, copies, mine):
            position = lax.axis_index(axis)
            before, everything = jnp.zeros((DK, DK), f32), mine
            for kk in range(1, count):
                copies[kk - 1].wait_recv()
                value = recv[i * 3 + stage, kk - 1].astype(f32)
                sender = lax.rem(position + count - kk, count)
                before += jnp.where(earlier(sender, position), value, 0.0)
                everything += value
            return before, everything

        def plain(slot, value):
            send[slot, 0] = value.astype(bf16)
            return lambda p: send.at[slot, 0]

        ax = go("seq_1", nx, 0, 0, plain(0, loc[0]))
        bz = go("seq_2", nz, 1, 0, plain(3, loc[1]))
        before_a, row = collect("seq_1", nx, 0, 0, ax, loc[0])
        ay = go("seq_0", ny, 0, 1, plain(1, row))
        more, _ = collect("seq_0", ny, 0, 1, ay, row)
        before_a += more
        send[2, 0] = before_a.astype(bf16)
        send[2, 1] = (before_a + loc[0]).astype(bf16)
        az = go("seq_2", nz, 0, 2, lambda p: send.at[2, jnp.where(earlier(zh, p), 1, 0)])
        before_b, line = collect("seq_2", nz, 1, 0, bz, loc[1])
        bx = go("seq_1", nx, 1, 1, plain(4, line))
        more, plane = collect("seq_1", nx, 1, 1, bx, line)
        before_b += more
        by = go("seq_0", ny, 1, 2, plain(5, plane))
        more, _ = collect("seq_0", ny, 1, 2, by, plane)
        inc[1] = before_b + more
        _, whole = collect("seq_2", nz, 0, 2, az, before_a)
        inc[0] = whole

    def within_body(b, i, at, cols):
        within[b, i] = dot(sc[b, i], v[at, cols], NN)

    each_block(within_body)
    scan(0, False)

    for i in range(heads):
        loc[i] = jnp.zeros((DK, DK), f32)

    def forward_body(b, i, at, cols):
        prior16 = inc[i].astype(bf16)
        prior[b, i] = prior16
        inc[i] += st[b, i]
        mixed = within[b, i] + dot(q_ref[at, cols], prior16, NN)
        inverse = 1.0 / jnp.sqrt(jnp.mean(mixed * mixed, axis=-1, keepdims=True) + norm_eps)
        normed = mixed * inverse
        attn_ref[at, cols] = normed.astype(bf16)
        upstream = go_ref[at, cols].astype(f32)
        inner = jnp.mean(upstream * normed, axis=-1, keepdims=True)
        grad_mixed = ((upstream - normed * inner) * inverse).astype(bf16)
        gm[at, cols] = grad_mixed
        s = dot(q_ref[at, cols], grad_mixed, TN)
        gs[b, i] = s
        loc[i] += s

    each_block(forward_body)

    def backward_body(b, i, at, cols):
        grad_mixed = gm[at, cols]
        grad_scores = jnp.where(causal, dot(grad_mixed, v[at, cols], NT), 0.0).astype(bf16)
        grad_query = dot(grad_scores, k_ref[at, cols], NN) + dot(grad_mixed, prior[b, i], NT)
        gq_ref[at, cols] = grad_query.astype(bf16)
        gkp[b, i] = dot(grad_scores, q_ref[at, cols], TN)
        gvp[b, i] = dot(sc[b, i], grad_mixed, TN)

    each_block(backward_body)
    scan(1, True)

    @pl.loop(0, blocks)
    def _(step_back):
        b = blocks - 1 - step_back
        at = pl.ds(pl.multiple_of(b * BLOCK, BLOCK), BLOCK)
        for i in range(heads):
            cols = slice(i * DK, (i + 1) * DK)
            following16 = inc[i].astype(bf16)
            inc[i] += gs[b, i]
            grad_key = gkp[b, i] + dot(v[at, cols], following16, NT)
            gk_ref[at, cols] = grad_key.astype(bf16)
            grad_value = gvp[b, i] + dot(k_ref[at, cols], following16, NN)
            gvt[cols, at] = grad_value.T.astype(bf16)

    piece = nz * rows
    side = columns // 2

    @pl.loop(0, nl * 2)
    def _(h):
        term = dot(gvt[...], xg[h // 2, lax.rem(h, 2)], NN).astype(bf16)
        for t in range(feats // piece):
            p = h * (feats // piece) + t
            part = term[:, t * piece : (t + 1) * piece]
            pa[p] = part[:side]
            pb[lax.rem(p, nx) * ny + p // nx] = part[side:]

    a1 = exchange("seq_0", ny, lambda p: pa.at[pl.ds(p * nx, nx)], lambda kk: ra1.at[kk - 1], g_s.at[0], g_r.at[0])
    b1 = exchange("seq_1", nx, lambda p: pb.at[pl.ds(p * ny, ny)], lambda kk: rb1.at[kk - 1], g_s.at[1], g_r.at[1])
    sent += a1 + b1

    def summed_a(t):
        value = pa[yy * nx + t].astype(f32)
        for kk in range(ny - 1):
            value += ra1[kk, t].astype(f32)
        return value

    def summed_b(t):
        value = pb[xx * ny + t].astype(f32)
        for kk in range(nx - 1):
            value += rb1[kk, t].astype(f32)
        return value

    arrive(a1)

    @pl.loop(0, nx)
    def _(t):
        sa2[t] = summed_a(t).astype(bf16)

    a2 = exchange("seq_1", nx, lambda p: sa2.at[p], lambda kk: ra2.at[kk - 1], g_s.at[2], g_r.at[2])
    arrive(b1)

    @pl.loop(0, ny)
    def _(t):
        sb2[t] = summed_b(t).astype(bf16)

    b2 = exchange("seq_0", ny, lambda p: sb2.at[p], lambda kk: rb2.at[kk - 1], g_s.at[3], g_r.at[3])
    sent += a2 + b2
    final_a = summed_a(xx)
    arrive(a2)
    for kk in range(nx - 1):
        final_a += ra2[kk].astype(f32)
    tzf[:, :side] = final_a.T
    final_b = summed_b(yy)
    arrive(b2)
    for kk in range(ny - 1):
        final_b += rb2[kk].astype(f32)
    tzf[:, side:] = final_b.T
    tz[...] = tzf[...].astype(bf16)
    z3 = exchange(
        "seq_2", nz, lambda p: tz.at[pl.ds(pl.multiple_of(p * rows, rows), rows)], lambda kk: rz.at[kk - 1],
        g_s.at[4], g_r.at[4],
    )
    sent += z3
    result = tzf[pl.ds(pl.multiple_of(zh * rows, rows), rows)]
    arrive(z3)
    for kk in range(nz - 1):
        result += rz[kk].astype(f32)
    gl_ref[...] = result

    for copy in sent:
        copy.wait_send()

    @pl.loop(0, nl)
    def _(block):
        @pl.loop(0, CHUNKS)
        def _(j):
            side_copy(block, j, False).wait_send()

            @pl.when(jnp.logical_and(block <= zl, zl < nl - 1))
            def _():
                line_copy(block, j, True, False).wait_send()

            @pl.when(jnp.logical_and(block >= zl, zl > 0))
            def _():
                line_copy(block, j, False, False).wait_send()


def per_device(inputs, latent, queries, keys, grad_out):
    sizes = tuple(lax.axis_size(a) for a in (*SEQ, "head_0"))
    ny, nx, nz, nl = sizes
    tokens, feats = inputs.shape
    rows, columns = latent.shape
    heads, blocks = columns // DK, tokens // BLOCK
    seqs, everyone = ny * nx * nz, ny * nx * nz * rows
    side, piece = columns // 2, nz * rows
    dma = pltpu.SemaphoreType.DMA
    most = max(ny, nx, nz) - 1
    scratch = [
        pltpu.VMEM((seqs, rows // 2, columns), bf16),
        pltpu.VMEM((seqs, rows // 2, columns), bf16),
        pltpu.VMEM((everyone, columns), bf16),
        pltpu.VMEM((nl, 2, tokens, feats), bf16),
        pltpu.VMEM((tokens, columns), f32),
        pltpu.VMEM((tokens, columns), bf16),
        pltpu.VMEM((blocks, heads, BLOCK, BLOCK), bf16),
        pltpu.VMEM((blocks, heads, DK, DK), f32),
        pltpu.VMEM((blocks, heads, DK, DK), bf16),
        pltpu.VMEM((blocks, heads, BLOCK, DK), f32),
        pltpu.VMEM((tokens, columns), bf16),
        pltpu.VMEM((blocks, heads, DK, DK), f32),
        pltpu.VMEM((blocks, heads, BLOCK, DK), f32),
        pltpu.VMEM((blocks, heads, BLOCK, DK), f32),
        pltpu.VMEM((columns, tokens), bf16),
        pltpu.VMEM((heads, DK, DK), f32),
        pltpu.VMEM((2, 6, 2, DK, DK), bf16),
        pltpu.VMEM((2, 6, most, DK, DK), bf16),
        pltpu.VMEM((heads, DK, DK), f32),
        pltpu.VMEM((ny * nx, side, piece), bf16),
        pltpu.VMEM((ny * nx, side, piece), bf16),
        pltpu.VMEM((ny - 1, nx, side, piece), bf16),
        pltpu.VMEM((nx - 1, ny, side, piece), bf16),
        pltpu.VMEM((nx, side, piece), bf16),
        pltpu.VMEM((ny, side, piece), bf16),
        pltpu.VMEM((nx - 1, side, piece), bf16),
        pltpu.VMEM((ny - 1, side, piece), bf16),
        pltpu.VMEM((piece, columns), bf16),
        pltpu.VMEM((piece, columns), f32),
        pltpu.VMEM((nz - 1, rows, columns), bf16),
        dma,
        dma((2, most)), dma((2, most)),
        dma((2, most)), dma((2, most)),
        dma((2, most)), dma((2, most)),
        dma((nl, CHUNKS)), dma((nl, CHUNKS)), dma((nl, CHUNKS)),
        dma((nl, CHUNKS)), dma((nl, CHUNKS)),
        dma((2, 6, most)), dma((2, 6, most)),
        dma((5, most)), dma((5, most)),
    ]
    vmem = pl.BlockSpec(memory_space=pltpu.VMEM)
    like = jax.ShapeDtypeStruct(queries.shape, bf16)
    return pl.pallas_call(
        functools.partial(kernel, sizes),
        out_shape=(like, like, like, jax.ShapeDtypeStruct(latent.shape, f32)),
        in_specs=[vmem] * 5,
        out_specs=(vmem,) * 4,
        scratch_shapes=scratch,
        compiler_params=pltpu.CompilerParams(
            collective_id=0, has_side_effects=True, vmem_limit_bytes=56 << 20
        ),
    )(inputs, latent, queries, keys, grad_out)


def solution(mesh):
    torus = Mesh(mesh.devices.reshape(4, 4, 4, 4, 2), (*SEQ, *HEAD))
    placed = P(SEQ, HEAD)
    return jax.shard_map(
        per_device,
        mesh=torus,
        in_specs=(placed,) * 5,
        out_specs=(placed,) * 4,
        check_vma=False,
    )
```

```python
import functools

import jax
import jax.numpy as jnp
from jax import lax
from jax.experimental import pallas as pl
from jax.experimental.pallas import tpu as pltpu
from jax.sharding import Mesh
from jax.sharding import PartitionSpec as P

DK = 128
BLOCK = 128
HEAD = ("head_0", "head_1")
SEQ = ("seq_0", "seq_1", "seq_2")
ID = pl.DeviceIdType.MESH
CHUNKS = 4

absmean_eps = 1e-05
norm_eps = 1e-06

f32 = jnp.float32
bf16 = jnp.bfloat16


def dot(a, b, contract):
    return lax.dot_general(a, b, ((contract[:1], contract[1:]), ((), ())), preferred_element_type=f32)


NN, NT, TN = (1, 0), (1, 1), (0, 0)


def exchange(axis, count, source, target, send, recv):
    position = lax.axis_index(axis)
    copies = []
    for kk in range(1, count):
        peer = lax.rem(position + kk, count)
        copy = pltpu.make_async_remote_copy(
            src_ref=source(peer),
            dst_ref=target(kk),
            send_sem=send.at[kk - 1],
            recv_sem=recv.at[kk - 1],
            device_id={axis: peer},
            device_id_type=ID,
        )
        copy.start()
        copies.append(copy)
    return copies


def arrive(copies):
    for copy in copies:
        copy.wait_recv()


def kernel(
    sizes, x_in, latent_in, q_in, k_in, go_in, attn_out, gq_out, gk_out, gl_out,
    attn_ref, gq_ref, gk_ref, gl_ref, latent_ref, q_ref, k_ref, go_ref, wa, wb, wt, xg, acc, v, sc, st, prior, within, gm, gs, following, gkp, gvp, gvt, loc, scan_send, scan_recv, zr, inc,
    pa, pb, ra1, rb1, sa2, sb2, ra2, rb2, tz, tzf, rz,
    own_sem, out_sem, wz_s, wz_r, w2_s, w2_r, w3_s, w3_r, xp_s, xm_s, xs_s, xl_r, xs_r, scan_s, scan_r, zs_s, zs_r, g1_s, g1_r, g_s, g_r,
):
    ny, nx, nz, nl = sizes
    yy, xx, zh = (lax.axis_index(a) for a in SEQ)
    zl, cc = (lax.axis_index(a) for a in HEAD)
    tokens, feats = x_in.shape
    rows, columns = latent_ref.shape
    half = rows // 2
    heads = columns // DK
    blocks = tokens // BLOCK
    step = tokens // CHUNKS
    sent = []

    written = [
        pltpu.make_async_copy(attn_ref, attn_out, out_sem.at[0]),
        pltpu.make_async_copy(gq_ref, gq_out, out_sem.at[1]),
        pltpu.make_async_copy(gk_ref, gk_out, out_sem.at[2]),
        pltpu.make_async_copy(gl_ref, gl_out, out_sem.at[3]),
    ]
    fetches = [
        pltpu.make_async_copy(latent_in, latent_ref, own_sem.at[0]),
        pltpu.make_async_copy(x_in, xg.at[zl, cc], own_sem.at[1]),
        pltpu.make_async_copy(q_in, q_ref, own_sem.at[2]),
        pltpu.make_async_copy(k_in, k_ref, own_sem.at[3]),
        pltpu.make_async_copy(go_in, go_ref, own_sem.at[4]),
    ]
    for fetch in fetches:
        fetch.start()
    at_a = (yy * nx + xx) * nz
    at_b = (xx * ny + yy) * nz
    barrier = pltpu.get_barrier_semaphore()
    for axis, count in (("seq_2", nz), ("seq_1", nx), ("seq_0", ny), ("head_1", 2)):
        position = lax.axis_index(axis)
        for kk in range(1, count):
            pl.semaphore_signal(
                barrier, inc=1, device_id={axis: lax.rem(position + kk, count)}, device_id_type=ID
            )

    @pl.when(zl > 0)
    def _():
        pl.semaphore_signal(barrier, inc=1, device_id={"head_0": zl - 1}, device_id_type=ID)

    @pl.when(zl < nl - 1)
    def _():
        pl.semaphore_signal(barrier, inc=1, device_id={"head_0": zl + 1}, device_id_type=ID)

    fetches[0].wait()
    latent16 = latent_ref[...].astype(bf16)
    wa[at_a + zh] = latent16[:half]
    wb[at_b + zh] = latent16[half:]
    fetches[1].wait()
    partners = (nz - 1) + (nx - 1) + (ny - 1) + 1
    neighbours = jnp.where(zl > 0, 1, 0) + jnp.where(zl < nl - 1, 1, 0)
    pl.semaphore_wait(barrier, partners + neighbours)

    up, down = lax.rem(zh + 1, nz), lax.rem(zh + nz - 1, nz)
    opposite = lax.rem(zh + 2, nz)

    def z_copy(peer, source, target, send, recv):
        copy = pltpu.make_async_remote_copy(
            src_ref=source, dst_ref=target, send_sem=send, recv_sem=recv,
            device_id={"seq_2": peer}, device_id_type=ID,
        )
        copy.start()
        sent.append(copy)
        return copy

    wz = exchange("seq_2", nz, lambda p: wa.at[at_a + zh], lambda kk: wa.at[at_a + zh], wz_s.at[0], wz_r.at[0])
    wz += exchange("seq_2", nz, lambda p: wb.at[at_b + zh], lambda kk: wb.at[at_b + zh], wz_s.at[1], wz_r.at[1])
    sent += wz

    def rows_of(ref, j):
        return ref.at[pl.ds(pl.multiple_of(j * step, step), step)]

    def line_copy(block, j, up):
        place = rows_of(xg.at[block, cc], j)
        return pltpu.make_async_remote_copy(
            src_ref=place,
            dst_ref=place,
            send_sem=(xp_s if up else xm_s).at[block, j],
            recv_sem=xl_r.at[block, j],
            device_id={"head_0": zl + 1 if up else zl - 1},
            device_id_type=ID,
        )

    def side_copy(block, j):
        place = rows_of(xg.at[block, cc], j)
        return pltpu.make_async_remote_copy(
            src_ref=place,
            dst_ref=place,
            send_sem=xs_s.at[block, j],
            recv_sem=xs_r.at[block, j],
            device_id={"head_1": 1 - cc},
            device_id_type=ID,
        )

    @pl.loop(0, CHUNKS)
    def _(j):
        @pl.when(zl < nl - 1)
        def _():
            line_copy(zl, j, True).start()

        @pl.when(zl > 0)
        def _():
            line_copy(zl, j, False).start()

    @pl.loop(0, CHUNKS)
    def _(j):
        side_copy(zl, j).start()

    def relay(distance):
        @pl.loop(0, CHUNKS)
        def _(j):
            @pl.when(zl >= distance)
            def _():
                block = zl - distance
                line_copy(block, j, True).wait_recv()

                @pl.when(zl < nl - 1)
                def _():
                    line_copy(block, j, True).start()

                side_copy(block, j).start()

            @pl.when(zl + distance < nl)
            def _():
                block = zl + distance
                line_copy(block, j, False).wait_recv()

                @pl.when(zl > 0)
                def _():
                    line_copy(block, j, False).start()

                side_copy(block, j).start()

    causal = lax.broadcasted_iota(jnp.int32, (BLOCK, BLOCK), 0) >= lax.broadcasted_iota(
        jnp.int32, (BLOCK, BLOCK), 1
    )

    def unrolled(body, first, last):
        for b in range(first, last):
            for i in range(heads):
                body(b, i, slice(b * BLOCK, (b + 1) * BLOCK), slice(i * DK, (i + 1) * DK))

    def each_block(body):
        @pl.loop(0, blocks)
        def _(b):
            at = pl.ds(pl.multiple_of(b * BLOCK, BLOCK), BLOCK)
            for i in range(heads):
                body(b, i, at, slice(i * DK, (i + 1) * DK))

    def scores_body(b, i, at, cols):
        s = dot(q_ref[at, cols], k_ref[at, cols], NT)
        sc[b, i] = jnp.where(causal, s, 0.0).astype(bf16)

    for fetch in fetches[2:]:
        fetch.wait()
    each_block(scores_body)

    arrive(wz)
    mine_a = wa.at[pl.ds(at_a, nz)]
    mine_b = wb.at[pl.ds(at_b, nz)]
    w2a = exchange("seq_1", nx, lambda p: mine_a, lambda kk: mine_a, w2_s.at[0], w2_r.at[0])
    w2b = exchange("seq_0", ny, lambda p: mine_b, lambda kk: mine_b, w2_s.at[1], w2_r.at[1])
    sent += w2a + w2b
    relay(1)
    row_a = wa.at[pl.ds(yy * nx * nz, nx * nz)]
    row_b = wb.at[pl.ds(xx * ny * nz, ny * nz)]
    arrive(w2a)
    w3a = exchange("seq_0", ny, lambda p: row_a, lambda kk: row_a, w3_s.at[0], w3_r.at[0])
    arrive(w2b)
    w3b = exchange("seq_1", nx, lambda p: row_b, lambda kk: row_b, w3_s.at[1], w3_r.at[1])
    sent += w3a + w3b
    for distance in range(2, nl - 1):
        relay(distance)
    arrive(w3a)
    arrive(w3b)

    def magnitude(s, total):
        both = jnp.abs(wa[s].astype(f32)) + jnp.abs(wb[s].astype(f32))
        return total + both.reshape(half // 8, 8, columns).sum(axis=0)

    total = lax.fori_loop(0, ny * nx * nz, magnitude, jnp.zeros((8, columns), f32))
    scale = total.sum(axis=0, keepdims=True) / (ny * nx * nz * rows) + absmean_eps
    halfway = 0.5 * scale

    def ternary(w):
        w = w.astype(f32)
        return jnp.where(w > halfway, scale, jnp.where(w < -halfway, -scale, 0.0)).astype(bf16)

    @pl.loop(0, ny * nx)
    def _(p):
        other = lax.rem(p, nx) * ny + p // nx
        for z in range(nz):
            at = pl.multiple_of((p * nz + z) * rows, rows)
            wt[pl.ds(at, half)] = ternary(wa[p * nz + z])
            wt[pl.ds(pl.multiple_of(at + half, half), half)] = ternary(wb[other * nz + z])

    acc[...] = jnp.zeros_like(acc)

    def features(block, core):
        return wt[pl.ds(pl.multiple_of((block * 2 + core) * feats, feats), feats)]

    @pl.loop(0, nl)
    def _(block):
        @pl.when(jnp.abs(block - zl) < nl - 1)
        def _():
            @pl.loop(0, CHUNKS)
            def _(j):
                side_copy(block, j).wait_recv()

            @pl.loop(0, 2)
            def _(core):
                acc[...] += dot(xg[block, core], features(block, core), NN)

    @pl.when(jnp.logical_or(zl == 0, zl == nl - 1))
    def _():
        far = nl - 1 - zl

        @pl.loop(0, CHUNKS)
        def _(j):
            at = pl.ds(pl.multiple_of(j * step, step), step)
            line_copy(far, j, True).wait_recv()
            side_copy(far, j).start()
            acc[at] += dot(xg[far, cc, at], features(far, cc), NN)
            side_copy(far, j).wait_recv()
            acc[at] += dot(xg[far, 1 - cc, at], features(far, 1 - cc), NN)

    v[...] = acc[...].astype(bf16)

    totals = [jnp.zeros((DK, DK), f32)] * heads

    def state_body(b, i, at, cols):
        s = dot(k_ref[at, cols], v[at, cols], TN)
        st[b, i] = s
        totals[i] = totals[i] + s

    unrolled(state_body, 0, blocks)
    for i in range(heads):
        loc[i] = totals[i]

    def scan(which, reverse, works):
        def earlier(p, mine):
            return p > mine if reverse else p < mine

        send, recv = scan_send.at[which], scan_recv.at[which]

        def go(axis, count, i, stage, source):
            slot = i * 3 + stage
            copies = exchange(
                axis, count, source, lambda kk: recv.at[slot, kk - 1],
                scan_s.at[which, slot], scan_r.at[which, slot],
            )
            sent.extend(copies)
            return copies

        def collect(axis, count, i, stage, copies, mine):
            position = lax.axis_index(axis)
            before, everything = jnp.zeros((DK, DK), f32), mine
            for kk in range(1, count):
                copies[kk - 1].wait_recv()
                value = recv[i * 3 + stage, kk - 1].astype(f32)
                sender = lax.rem(position + count - kk, count)
                before += jnp.where(earlier(sender, position), value, 0.0)
                everything += value
            return before, everything

        def plain(slot, value):
            send[slot, 0] = value.astype(bf16)
            return lambda p: send.at[slot, 0]

        top, bottom = pl.ds(0, DK // 2), pl.ds(DK // 2, DK // 2)

        def step_z(peer, source, target, n):
            return z_copy(peer, source, target, zs_s.at[which, n], zs_r.at[which, n])

        ax = go("seq_1", nx, 0, 0, plain(0, loc[0]))
        send[3, 0] = loc[1].astype(bf16)
        from_z = zr.at[which, 0]
        bz = [
            step_z(up, send.at[3, 0], from_z.at[0], 0),
            step_z(down, send.at[3, 0], from_z.at[1], 1),
            step_z(opposite, send.at[3, 0], from_z.at[2], 2),
        ]
        works[0]()
        before_a, row = collect("seq_1", nx, 0, 0, ax, loc[0])
        ay = go("seq_0", ny, 0, 1, plain(1, row))
        works[1]()
        more, _ = collect("seq_0", ny, 0, 1, ay, row)
        before_a += more
        send[2, 0] = before_a.astype(bf16)
        send[2, 1] = (before_a + loc[0]).astype(bf16)

        def message(peer):
            return send.at[2, jnp.where(earlier(zh, peer), 1, 0)]

        to_z = zr.at[which, 1]
        az = [
            step_z(up, message(opposite).at[top], to_z.at[2, top], 4),
            step_z(down, message(opposite).at[bottom], to_z.at[2, bottom], 5),
            step_z(up, message(up).at[bottom], to_z.at[0, bottom], 6),
            step_z(down, message(down).at[top], to_z.at[1, top], 7),
        ]
        before_b, line = jnp.zeros((DK, DK), f32), loc[1]
        arrive(bz)
        for n, sender in ((0, down), (1, up), (2, opposite)):
            value = from_z[n].astype(f32)
            before_b += jnp.where(earlier(sender, zh), value, 0.0)
            line += value
        bx = go("seq_1", nx, 1, 1, plain(4, line))
        half_rows = DK // 2
        az[0].wait_recv()
        send[5, 1, :half_rows] = (to_z[2, :half_rows].astype(f32) + message(up)[:half_rows].astype(f32)).astype(bf16)
        az += [step_z(up, send.at[5, 1, top], to_z.at[0, top], 8)]
        az[1].wait_recv()
        send[5, 1, half_rows:] = (to_z[2, half_rows:].astype(f32) + message(down)[half_rows:].astype(f32)).astype(bf16)
        az += [step_z(down, send.at[5, 1, bottom], to_z.at[1, bottom], 9)]
        more, plane = collect("seq_1", nx, 1, 1, bx, line)
        before_b += more
        by = go("seq_0", ny, 1, 2, plain(5, plane))
        more, _ = collect("seq_0", ny, 1, 2, by, plane)
        inc[1] = before_b + more
        arrive(az[2:])
        inc[0] = before_a + to_z[0].astype(f32) + to_z[1].astype(f32)

    def within_body(b, i, at, cols):
        within[b, i] = dot(sc[b, i], v[at, cols], NN)

    halfway_block = blocks // 2
    scan(
        0, False,
        (lambda: unrolled(within_body, 0, halfway_block), lambda: unrolled(within_body, halfway_block, blocks)),
    )

    for i in range(heads):
        loc[i] = jnp.zeros((DK, DK), f32)

    def forward_body(b, i, at, cols):
        prior16 = inc[i].astype(bf16)
        prior[b, i] = prior16
        inc[i] += st[b, i]
        mixed = within[b, i] + dot(q_ref[at, cols], prior16, NN)
        inverse = 1.0 / jnp.sqrt(jnp.mean(mixed * mixed, axis=-1, keepdims=True) + norm_eps)
        normed = mixed * inverse
        attn_ref[at, cols] = normed.astype(bf16)
        upstream = go_ref[at, cols].astype(f32)
        inner = jnp.mean(upstream * normed, axis=-1, keepdims=True)
        grad_mixed = ((upstream - normed * inner) * inverse).astype(bf16)
        gm[at, cols] = grad_mixed
        s = dot(q_ref[at, cols], grad_mixed, TN)
        gs[b, i] = s
        loc[i] += s

    each_block(forward_body)
    written[0].start()

    def backward_body(b, i, at, cols):
        grad_mixed = gm[at, cols]
        grad_scores = jnp.where(causal, dot(grad_mixed, v[at, cols], NT), 0.0).astype(bf16)
        grad_query = dot(grad_scores, k_ref[at, cols], NN) + dot(grad_mixed, prior[b, i], NT)
        gq_ref[at, cols] = grad_query.astype(bf16)
        gkp[b, i] = dot(grad_scores, q_ref[at, cols], TN)
        gvp[b, i] = dot(sc[b, i], grad_mixed, TN)

    scan(
        1, True,
        (lambda: unrolled(backward_body, 0, halfway_block), lambda: unrolled(backward_body, halfway_block, blocks)),
    )

    written[1].start()
    carried = [inc[i] for i in range(heads)]
    for b in reversed(range(blocks)):
        at = slice(b * BLOCK, (b + 1) * BLOCK)
        for i in range(heads):
            cols = slice(i * DK, (i + 1) * DK)
            following16 = carried[i].astype(bf16)
            following[b, i] = following16
            carried[i] = carried[i] + gs[b, i]
            grad_value = gvp[b, i] + dot(k_ref[at, cols], following16, NN)
            gvt[cols, at] = grad_value.T.astype(bf16)

    piece = nz * rows
    side = columns // 2

    per_block = feats // piece
    order = []
    for k in (2, 1, 3, 0):
        order += [(dy, k) for dy in (2, 1, 3, 0)] + [(k, dx) for dx in (2, 1, 3, 0)]
    half_side = side // 2
    first, second_half = slice(0, half_side), slice(half_side, side)
    ring = {}

    def hop(which, k, n, forward, source, target):
        axis, position, count = (("seq_0", yy, ny), ("seq_1", xx, nx))[which]
        peer = lax.rem(position + (1 if forward else count - 1), count)
        copy = pltpu.make_async_remote_copy(
            src_ref=source, dst_ref=target,
            send_sem=g1_s.at[which, k, n], recv_sem=g1_r.at[which, k, n],
            device_id={axis: peer}, device_id_type=ID,
        )
        copy.start()
        sent.append(copy)
        ring[which, k, n] = copy

    def begin(which, distance, k, source, target):
        if distance == 2:
            hop(which, k, 0, True, source.at[first], target.at[2, k, first])
            hop(which, k, 1, False, source.at[second_half], target.at[2, k, second_half])
        elif distance == 1:
            hop(which, k, 2, True, source.at[second_half], target.at[0, k, second_half])
        elif distance == 3:
            hop(which, k, 3, False, source.at[first], target.at[1, k, first])

    def pass_on(which, k, ahead, behind, target):
        ring[which, k, 0].wait_recv()
        ahead[first] = (ahead[first].astype(f32) + target[2, k, first].astype(f32)).astype(bf16)
        hop(which, k, 4, True, ahead.at[first], target.at[0, k, first])
        ring[which, k, 1].wait_recv()
        behind[second_half] = (behind[second_half].astype(f32) + target[2, k, second_half].astype(f32)).astype(bf16)
        hop(which, k, 5, False, behind.at[second_half], target.at[1, k, second_half])

    def pass_both(k):
        pass_on(0, k, pa.at[1, k], pa.at[3, k], ra1)
        pass_on(1, k, pb.at[k, 1], pb.at[k, 3], rb1)

    for n, (dy, dx) in enumerate(dict.fromkeys(order)):
        to_y, to_x = lax.rem(yy + dy, ny), lax.rem(xx + dx, nx)
        p = to_y * nx + to_x
        block = p // per_block
        lanes = pl.ds(pl.multiple_of(lax.rem(p, per_block) * piece, piece), piece)
        term = dot(gvt[...], xg[block // 2, lax.rem(block, 2), :, lanes], NN).astype(bf16)
        pa[dy, dx] = term[:side]
        pb[dy, dx] = term[side:]
        begin(0, dy, dx, pa.at[dy, dx], ra1)
        begin(1, dx, dy, pb.at[dy, dx], rb1)
        if n == 11:
            pass_both(2)
    for k in (1, 3, 0):
        pass_both(k)

    def key_body(b, i, at, cols):
        grad_key = gkp[b, i] + dot(v[at, cols], following[b, i], NT)
        gk_ref[at, cols] = grad_key.astype(bf16)

    each_block(key_body)
    written[2].start()

    def summed_a(dx):
        value = pa[0, dx].astype(f32)
        for n in (2, 3, 4, 5):
            ring[0, dx, n].wait_recv()
        return value + ra1[0, dx].astype(f32) + ra1[1, dx].astype(f32)

    def summed_b(dy):
        value = pb[dy, 0].astype(f32)
        for n in (2, 3, 4, 5):
            ring[1, dy, n].wait_recv()
        return value + rb1[0, dy].astype(f32) + rb1[1, dy].astype(f32)

    def second(axis, position, count, k, source, target, which):
        copy = pltpu.make_async_remote_copy(
            src_ref=source.at[k - 1], dst_ref=target.at[k - 1],
            send_sem=g_s.at[which, k - 1], recv_sem=g_r.at[which, k - 1],
            device_id={axis: lax.rem(position + k, count)}, device_id_type=ID,
        )
        copy.start()
        sent.append(copy)
        return copy

    a2, b2 = [], []
    for k in (2, 1, 3):
        if k < nx:
            sa2[k - 1] = summed_a(k).astype(bf16)
            a2.append(second("seq_1", xx, nx, k, sa2, ra2, 0))
        if k < ny:
            sb2[k - 1] = summed_b(k).astype(bf16)
            b2.append(second("seq_0", yy, ny, k, sb2, rb2, 1))
    final_a, final_b = summed_a(0), summed_b(0)

    def last(final, second_copies, received, which):
        for copy in second_copies:
            copy.wait_recv()
        for kk in range(len(second_copies)):
            final += received[kk].astype(f32)
        final = final.T
        tzf[which] = final
        tz[which] = final.astype(bf16)
        return exchange(
            "seq_2", nz, lambda p: tz.at[which, pl.ds(pl.multiple_of(p * rows, rows), rows)],
            lambda kk: rz.at[which, kk - 1], g_s.at[2 + which], g_r.at[2 + which],
        )

    z3 = [last(final_a, a2, ra2, 0), last(final_b, b2, rb2, 1)]
    for which, copies in enumerate(z3):
        sent += copies
        result = tzf[which, pl.ds(pl.multiple_of(zh * rows, rows), rows)]
        arrive(copies)
        for kk in range(nz - 1):
            result += rz[which, kk].astype(f32)
        gl_ref[:, which * side : (which + 1) * side] = result

    written[3].start()
    for copy in sent:
        copy.wait_send()
    for copy in written:
        copy.wait()

    @pl.loop(0, nl)
    def _(block):
        @pl.loop(0, CHUNKS)
        def _(j):
            side_copy(block, j).wait_send()

            @pl.when(jnp.logical_and(block <= zl, zl < nl - 1))
            def _():
                line_copy(block, j, True).wait_send()

            @pl.when(jnp.logical_and(block >= zl, zl > 0))
            def _():
                line_copy(block, j, False).wait_send()


def deliver(*refs):
    sems = refs[12]
    inward = [pltpu.make_async_copy(refs[i], refs[8 + i], sems.at[0, i]) for i in range(4)]
    outward = [pltpu.make_async_copy(refs[8 + i], refs[4 + i], sems.at[1, i]) for i in range(4)]
    for copy in inward:
        copy.start()
    for copy, following in zip(inward, outward):
        copy.wait()
        following.start()
    for copy in outward:
        copy.wait()


def per_device(inputs, latent, queries, keys, grad_out):
    sizes = tuple(lax.axis_size(a) for a in (*SEQ, "head_0"))
    ny, nx, nz, nl = sizes
    tokens, feats = inputs.shape
    rows, columns = latent.shape
    heads, blocks = columns // DK, tokens // BLOCK
    seqs, everyone = ny * nx * nz, ny * nx * nz * rows
    side, piece = columns // 2, nz * rows
    dma = pltpu.SemaphoreType.DMA
    most = max(ny, nx, nz) - 1
    scratch = [
        *[pltpu.VMEM((tokens, columns), bf16)] * 3,
        pltpu.VMEM(latent.shape, f32),
        pltpu.VMEM(latent.shape, f32),
        pltpu.VMEM((tokens, columns), bf16),
        pltpu.VMEM((tokens, columns), bf16),
        pltpu.VMEM((tokens, columns), bf16),
        pltpu.VMEM((seqs, rows // 2, columns), bf16),
        pltpu.VMEM((seqs, rows // 2, columns), bf16),
        pltpu.VMEM((everyone, columns), bf16),
        pltpu.VMEM((nl, 2, tokens, feats), bf16),
        pltpu.VMEM((tokens, columns), f32),
        pltpu.VMEM((tokens, columns), bf16),
        pltpu.VMEM((blocks, heads, BLOCK, BLOCK), bf16),
        pltpu.VMEM((blocks, heads, DK, DK), f32),
        pltpu.VMEM((blocks, heads, DK, DK), bf16),
        pltpu.VMEM((blocks, heads, BLOCK, DK), f32),
        pltpu.VMEM((tokens, columns), bf16),
        pltpu.VMEM((blocks, heads, DK, DK), f32),
        pltpu.VMEM((blocks, heads, DK, DK), bf16),
        pltpu.VMEM((blocks, heads, BLOCK, DK), f32),
        pltpu.VMEM((blocks, heads, BLOCK, DK), f32),
        pltpu.VMEM((columns, tokens), bf16),
        pltpu.VMEM((heads, DK, DK), f32),
        pltpu.VMEM((2, 6, 2, DK, DK), bf16),
        pltpu.VMEM((2, 6, most, DK, DK), bf16),
        pltpu.VMEM((2, 2, 3, DK, DK), bf16),
        pltpu.VMEM((heads, DK, DK), f32),
        pltpu.VMEM((ny, nx, side, piece), bf16),
        pltpu.VMEM((ny, nx, side, piece), bf16),
        pltpu.VMEM((ny - 1, nx, side, piece), bf16),
        pltpu.VMEM((nx - 1, ny, side, piece), bf16),
        pltpu.VMEM((nx - 1, side, piece), bf16),
        pltpu.VMEM((ny - 1, side, piece), bf16),
        pltpu.VMEM((nx - 1, side, piece), bf16),
        pltpu.VMEM((ny - 1, side, piece), bf16),
        pltpu.VMEM((2, piece, side), bf16),
        pltpu.VMEM((2, piece, side), f32),
        pltpu.VMEM((2, nz - 1, rows, side), bf16),
        dma((5,)),
        dma((4,)),
        dma((2, most)), dma((2, most)),
        dma((2, most)), dma((2, most)),
        dma((2, most)), dma((2, most)),
        dma((nl, CHUNKS)), dma((nl, CHUNKS)), dma((nl, CHUNKS)),
        dma((nl, CHUNKS)), dma((nl, CHUNKS)),
        dma((2, 6, most)), dma((2, 6, most)),
        dma((2, 10)), dma((2, 10)),
        dma((2, 4, 6)), dma((2, 4, 6)),
        dma((4, most)), dma((4, most)),
    ]
    like = jax.ShapeDtypeStruct(queries.shape, bf16)
    results = pl.pallas_call(
        functools.partial(kernel, sizes),
        out_shape=(like, like, like, jax.ShapeDtypeStruct(latent.shape, f32)),
        in_specs=[pl.BlockSpec(memory_space=pltpu.HBM)] * 5,
        out_specs=(pl.BlockSpec(memory_space=pltpu.HBM),) * 4,
        scratch_shapes=scratch,
        compiler_params=pltpu.CompilerParams(
            collective_id=0, has_side_effects=True, vmem_limit_bytes=60 << 20
        ),
    )(inputs, latent, queries, keys, grad_out)
    return pl.pallas_call(
        deliver,
        out_shape=(like, like, like, jax.ShapeDtypeStruct(latent.shape, f32)),
        in_specs=[pl.BlockSpec(memory_space=pltpu.HBM)] * 4,
        out_specs=(pl.BlockSpec(memory_space=pltpu.HBM),) * 4,
        scratch_shapes=[
            *[pltpu.VMEM(queries.shape, bf16)] * 3,
            pltpu.VMEM(latent.shape, f32),
            pltpu.SemaphoreType.DMA((2, 4)),
        ],
        compiler_params=pltpu.CompilerParams(vmem_limit_bytes=60 << 20),
    )(*results)


def solution(mesh):
    torus = Mesh(mesh.devices.reshape(4, 4, 4, 4, 2), (*SEQ, *HEAD))
    placed = P(SEQ, HEAD)
    return jax.shard_map(
        per_device,
        mesh=torus,
        in_specs=(placed,) * 5,
        out_specs=(placed,) * 4,
        check_vma=False,
    )
```

```python
import functools
import itertools

import jax
import jax.numpy as jnp
from jax import lax
from jax.experimental import pallas as pl
from jax.experimental.pallas import tpu as pltpu
from jax.sharding import Mesh
from jax.sharding import PartitionSpec as P

DK = 128
BLOCK = 128
HEAD = ("head_0", "head_1")
SEQ = ("seq_0", "seq_1", "seq_2")
ID = pl.DeviceIdType.MESH
CHUNKS = 8
EARLY = 3

absmean_eps = 1e-05
norm_eps = 1e-06

f32 = jnp.float32
bf16 = jnp.bfloat16


def dot(a, b, contract):
    return lax.dot_general(a, b, ((contract[:1], contract[1:]), ((), ())), preferred_element_type=f32)


NN, NT, TN = (1, 0), (1, 1), (0, 0)


def exchange(axis, count, source, target, send, recv):
    position = lax.axis_index(axis)
    copies = []
    for kk in range(1, count):
        peer = lax.rem(position + kk, count)
        copy = pltpu.make_async_remote_copy(
            src_ref=source(peer),
            dst_ref=target(kk),
            send_sem=send.at[kk - 1],
            recv_sem=recv.at[kk - 1],
            device_id={axis: peer},
            device_id_type=ID,
        )
        copy.start()
        copies.append(copy)
    return copies


def arrive(copies):
    for copy in copies:
        copy.wait_recv()


def kernel(
    sizes, x_in, latent_in, q_in, k_in, go_in, attn_ref, gq_ref, gk_ref, gl_ref,
    latent_ref, q_ref, k_ref, go_ref, wa, wb, wt, xg, acc, v, sc, st, prior, within, gm, gs, following, gkp, gvp, gvt, loc, scan_send, scan_recv, zr, inc,
    pa, pb, ra1, rb1, sa2, sb2, ra2, rb2, tz, tzf, rz,
    own_sem, wz_s, wz_r, w2_s, w2_r, w3_s, w3_r, xp_s, xm_s, xs_s, xl_r, xs_r, scan_s, scan_r, zs_s, zs_r, g1_s, g1_r, g_s, g_r,
):
    ny, nx, nz, nl = sizes
    yy, xx, zh = (lax.axis_index(a) for a in SEQ)
    zl, cc = (lax.axis_index(a) for a in HEAD)
    tokens, feats = x_in.shape
    rows, columns = latent_ref.shape
    half = rows // 2
    heads = columns // DK
    blocks = tokens // BLOCK
    step = tokens // CHUNKS
    sent = []

    fetches = [
        pltpu.make_async_copy(latent_in, latent_ref, own_sem.at[0]),
        pltpu.make_async_copy(x_in, xg.at[zl, cc], own_sem.at[1]),
        pltpu.make_async_copy(q_in, q_ref, own_sem.at[2]),
        pltpu.make_async_copy(k_in, k_ref, own_sem.at[3]),
        pltpu.make_async_copy(go_in, go_ref, own_sem.at[4]),
    ]
    for fetch in fetches:
        fetch.start()
    at_a = (yy * nx + xx) * nz
    at_b = (xx * ny + yy) * nz
    barrier = pltpu.get_barrier_semaphore()
    for axis, count in (("seq_2", nz), ("seq_1", nx), ("seq_0", ny), ("head_1", 2)):
        position = lax.axis_index(axis)
        for kk in range(1, count):
            pl.semaphore_signal(
                barrier, inc=1, device_id={axis: lax.rem(position + kk, count)}, device_id_type=ID
            )

    @pl.when(zl > 0)
    def _():
        pl.semaphore_signal(barrier, inc=1, device_id={"head_0": zl - 1}, device_id_type=ID)

    @pl.when(zl < nl - 1)
    def _():
        pl.semaphore_signal(barrier, inc=1, device_id={"head_0": zl + 1}, device_id_type=ID)

    fetches[0].wait()
    latent16 = latent_ref[...].astype(bf16)
    wa[at_a + zh] = latent16[:half]
    wb[at_b + zh] = latent16[half:]
    fetches[1].wait()
    partners = (nz - 1) + (nx - 1) + (ny - 1) + 1
    neighbours = jnp.where(zl > 0, 1, 0) + jnp.where(zl < nl - 1, 1, 0)
    pl.semaphore_wait(barrier, partners + neighbours)

    up, down = lax.rem(zh + 1, nz), lax.rem(zh + nz - 1, nz)
    opposite = lax.rem(zh + 2, nz)

    def z_copy(peer, source, target, send, recv):
        copy = pltpu.make_async_remote_copy(
            src_ref=source, dst_ref=target, send_sem=send, recv_sem=recv,
            device_id={"seq_2": peer}, device_id_type=ID,
        )
        copy.start()
        sent.append(copy)
        return copy

    def w_copy(peer, ref, at, n):
        return z_copy(peer, ref.at[at], ref.at[at], wz_s.at[n], wz_r.at[n])

    wz = [
        w_copy(up, wa, at_a + zh, 0),
        w_copy(down, wb, at_b + zh, 1),
        w_copy(up, wb, at_b + zh, 2),
        w_copy(down, wa, at_a + zh, 3),
    ]

    def rows_of(ref, j):
        return ref.at[pl.ds(pl.multiple_of(j * step, step), step)]

    def line_copy(block, j, up):
        place = rows_of(xg.at[block, cc], j)
        return pltpu.make_async_remote_copy(
            src_ref=place,
            dst_ref=place,
            send_sem=(xp_s if up else xm_s).at[block, j],
            recv_sem=xl_r.at[block, j],
            device_id={"head_0": zl + 1 if up else zl - 1},
            device_id_type=ID,
        )

    def side_copy(block, j):
        place = rows_of(xg.at[block, cc], j)
        return pltpu.make_async_remote_copy(
            src_ref=place,
            dst_ref=place,
            send_sem=xs_s.at[block, j],
            recv_sem=xs_r.at[block, j],
            device_id={"head_1": 1 - cc},
            device_id_type=ID,
        )

    def send_own(first, last):
        @pl.loop(first, last)
        def _(j):
            @pl.when(zl < nl - 1)
            def _():
                line_copy(zl, j, True).start()

            @pl.when(zl > 0)
            def _():
                line_copy(zl, j, False).start()

            side_copy(zl, j).start()

    send_own(0, EARLY)

    def relay(distance, first, last):
        @pl.loop(first, last)
        def _(j):
            @pl.when(zl >= distance)
            def _():
                block = zl - distance
                line_copy(block, j, True).wait_recv()

                @pl.when(zl < nl - 1)
                def _():
                    line_copy(block, j, True).start()

                side_copy(block, j).start()

            @pl.when(zl + distance < nl)
            def _():
                block = zl + distance
                line_copy(block, j, False).wait_recv()

                @pl.when(zl > 0)
                def _():
                    line_copy(block, j, False).start()

                side_copy(block, j).start()

    causal = lax.broadcasted_iota(jnp.int32, (BLOCK, BLOCK), 0) >= lax.broadcasted_iota(
        jnp.int32, (BLOCK, BLOCK), 1
    )

    def unrolled(body, first, last):
        for b in range(first, last):
            for i in range(heads):
                body(b, i, slice(b * BLOCK, (b + 1) * BLOCK), slice(i * DK, (i + 1) * DK))

    def each_block(body):
        @pl.loop(0, blocks)
        def _(b):
            at = pl.ds(pl.multiple_of(b * BLOCK, BLOCK), BLOCK)
            for i in range(heads):
                body(b, i, at, slice(i * DK, (i + 1) * DK))

    def scores_body(b, i, at, cols):
        s = dot(q_ref[at, cols], k_ref[at, cols], NT)
        sc[b, i] = jnp.where(causal, s, 0.0).astype(bf16)

    for fetch in fetches[2:]:
        fetch.wait()
    each_block(scores_body)

    wz[0].wait_recv()
    wz += [w_copy(up, wa, at_a + down, 4)]
    wz[1].wait_recv()
    wz += [w_copy(down, wb, at_b + up, 5)]
    send_own(EARLY, CHUNKS)
    relay(1, 0, CHUNKS // 2)
    arrive(wz[2:])
    mine_a = wa.at[pl.ds(at_a, nz)]
    mine_b = wb.at[pl.ds(at_b, nz)]
    w2a = exchange("seq_1", nx, lambda p: mine_a, lambda kk: mine_a, w2_s.at[0], w2_r.at[0])
    w2b = exchange("seq_0", ny, lambda p: mine_b, lambda kk: mine_b, w2_s.at[1], w2_r.at[1])
    sent += w2a + w2b
    relay(1, CHUNKS // 2, CHUNKS)
    row_a = wa.at[pl.ds(yy * nx * nz, nx * nz)]
    row_b = wb.at[pl.ds(xx * ny * nz, ny * nz)]
    arrive(w2a)
    w3a = exchange("seq_0", ny, lambda p: row_a, lambda kk: row_a, w3_s.at[0], w3_r.at[0])
    arrive(w2b)
    w3b = exchange("seq_1", nx, lambda p: row_b, lambda kk: row_b, w3_s.at[1], w3_r.at[1])
    sent += w3a + w3b
    for distance in range(2, nl - 1):
        relay(distance, 0, CHUNKS)
    arrive(w3a)
    arrive(w3b)
    far = nl - 1 - zl

    def at_end(body):
        pl.when(jnp.logical_or(zl == 0, zl == nl - 1))(body)

    def share_far(first, last):
        @at_end
        def _():
            @pl.loop(first, last)
            def _(j):
                line_copy(far, j, True).wait_recv()
                side_copy(far, j).start()

    share_far(0, 2)

    def magnitude(s, total):
        both = jnp.abs(wa[s].astype(f32)) + jnp.abs(wb[s].astype(f32))
        return total + both.reshape(half // 8, 8, columns).sum(axis=0)

    total = lax.fori_loop(0, ny * nx * nz, magnitude, jnp.zeros((8, columns), f32))
    scale = total.sum(axis=0, keepdims=True) / (ny * nx * nz * rows) + absmean_eps
    halfway = 0.5 * scale

    def ternary(w):
        w = w.astype(f32)
        return jnp.where(w > halfway, scale, jnp.where(w < -halfway, -scale, 0.0)).astype(bf16)

    @pl.loop(0, ny * nx)
    def _(p):
        other = lax.rem(p, nx) * ny + p // nx
        for z in range(nz):
            at = pl.multiple_of((p * nz + z) * rows, rows)
            wt[pl.ds(at, half)] = ternary(wa[p * nz + z])
            wt[pl.ds(pl.multiple_of(at + half, half), half)] = ternary(wb[other * nz + z])

    share_far(2, 3)
    acc[...] = jnp.zeros_like(acc)

    def features(block, core):
        return wt[pl.ds(pl.multiple_of((block * 2 + core) * feats, feats), feats)]

    @pl.loop(0, nl)
    def _(block):
        @pl.when(jnp.abs(block - zl) < nl - 1)
        def _():
            @pl.loop(0, CHUNKS)
            def _(j):
                side_copy(block, j).wait_recv()

            @pl.loop(0, 2)
            def _(core):
                acc[...] += dot(xg[block, core], features(block, core), NN)

    share_far(3, CHUNKS // 2 + 1)

    @at_end
    def _():
        half_at = pl.ds(0, tokens // 2)

        @pl.loop(0, CHUNKS // 2)
        def _(j):
            side_copy(far, j).wait_recv()

        acc[half_at] += dot(xg[far, cc, half_at], features(far, cc), NN)
        acc[half_at] += dot(xg[far, 1 - cc, half_at], features(far, 1 - cc), NN)

        def multiply(core, j):
            at = slice(j * step, (j + 1) * step)
            acc[at] += dot(xg[far, core, at], features(far, core), NN)

        for j in range(CHUNKS // 2, CHUNKS):
            if j > CHUNKS // 2:
                line_copy(far, j, True).wait_recv()
                side_copy(far, j).start()
                side_copy(far, j - 1).wait_recv()
                multiply(1 - cc, j - 1)
            multiply(cc, j)
        side_copy(far, CHUNKS - 1).wait_recv()
        multiply(1 - cc, CHUNKS - 1)

    v[...] = acc[...].astype(bf16)

    totals = [jnp.zeros((DK, DK), f32)] * heads

    def state_body(b, i, at, cols):
        s = dot(k_ref[at, cols], v[at, cols], TN)
        st[b, i] = s
        totals[i] = totals[i] + s

    unrolled(state_body, 0, blocks)
    for i in range(heads):
        loc[i] = totals[i]

    part = DK // 2
    tasks, serial = [], itertools.count()
    finished = {}

    def exchange_part(axis, count, which, i, r, stage, slot):
        copies = exchange(
            axis, count, lambda p: scan_send.at[which, i, r, slot], lambda kk: scan_recv.at[which, i, r, stage, kk - 1],
            scan_s.at[which, i, r, stage], scan_r.at[which, i, r, stage],
        )
        sent.extend(copies)
        return copies

    def collect(axis, count, which, i, r, stage, copies, mine):
        position = lax.axis_index(axis)
        before, everything = jnp.zeros((part, DK), f32), mine
        for kk in range(1, count):
            copies[kk - 1].wait_recv()
            value = scan_recv[which, i, r, stage, kk - 1].astype(f32)
            sender = lax.rem(position + count - kk, count)
            before += jnp.where(earlier(which, sender, position), value, 0.0)
            everything += value
        return before, everything

    def earlier(which, p, mine):
        return p > mine if which else p < mine

    def step_z(which, i, r, n, peer, source, target):
        return z_copy(peer, source, target, zs_s.at[which, i, r, n], zs_r.at[which, i, r, n])

    def chain_xyz(which, i, r, now):
        send, arrived = scan_send.at[which, i, r], zr.at[which, i, r]
        own = slice(r * part, (r + 1) * part)
        value = loc[i, own]
        send[0] = value.astype(bf16)
        copies = exchange_part("seq_1", nx, which, i, r, 0, 0)
        yield now + 3.3
        before, row = collect("seq_1", nx, which, i, r, 0, copies, value)
        send[1] = row.astype(bf16)
        copies = exchange_part("seq_0", ny, which, i, r, 1, 1)
        yield now + 6.4
        more, _ = collect("seq_0", ny, which, i, r, 1, copies, row)
        before += more
        send[2] = before.astype(bf16)
        send[3] = (before + loc[i, own]).astype(bf16)

        def message(peer):
            return send.at[2 + jnp.where(earlier(which, zh, peer), 1, 0)]

        az = [
            step_z(which, i, r, n, peer, message(peer), arrived.at[n])
            for n, peer in ((0, opposite), (1, up), (2, down))
        ]
        yield now + 14.4
        arrive(az)
        inc[i, own] = before + arrived[0].astype(f32) + arrived[1].astype(f32) + arrived[2].astype(f32)
        done(which, now + 14.4)

    def chain_zxy(which, i, r, now):
        send, arrived = scan_send.at[which, i, r], zr.at[which, i, r]
        own = slice(r * part, (r + 1) * part)
        send[0] = loc[i, own].astype(bf16)
        bz = [
            step_z(which, i, r, 0, up, send.at[0], arrived.at[0]),
            step_z(which, i, r, 1, down, send.at[0], arrived.at[1]),
            step_z(which, i, r, 2, opposite, send.at[0], arrived.at[2]),
        ]
        yield now + 8.0
        before, line = jnp.zeros((part, DK), f32), loc[i, own]
        for n, sender in ((0, down), (1, up), (2, opposite)):
            bz[n].wait_recv()
            value = arrived[n].astype(f32)
            before += jnp.where(earlier(which, sender, zh), value, 0.0)
            line += value
        send[1] = line.astype(bf16)
        copies = exchange_part("seq_1", nx, which, i, r, 0, 1)
        yield now + 11.3
        more, plane = collect("seq_1", nx, which, i, r, 0, copies, line)
        before += more
        send[2] = plane.astype(bf16)
        copies = exchange_part("seq_0", ny, which, i, r, 1, 2)
        yield now + 14.6
        more, _ = collect("seq_0", ny, which, i, r, 1, copies, plane)
        inc[i, own] = before + more
        done(which, now + 14.6)

    def begin_scan(which, i, now):
        for r in range(2):
            chain = chain_zxy if i % 2 else chain_xyz
            tasks.append((now + 0.01 * r, next(serial), chain(which, i, r, now + 0.5 * r)))

    def work(body, i, first, last):
        for b in range(first, last):
            body(b, i, slice(b * BLOCK, (b + 1) * BLOCK), slice(i * DK, (i + 1) * DK))
        return
        yield

    def later(now, body, i):
        for t in range(2):
            tasks.append((now + 0.7 * t, next(serial), work(body, i, blocks // 2 * t, blocks // 2 * (t + 1))))

    def done(which, now):
        finished[which] = finished.get(which, 0) + 1
        if finished[which] < 2 * heads:
            return
        if which:
            for i in range(heads):
                follow(i)
            return
        forward()
        for i in reversed(range(heads)):
            begin_scan(1, i, now + 2.0)
        for i in range(heads):
            later(now + 2.1, backward_body, i)

    def within_body(b, i, at, cols):
        within[b, i] = dot(sc[b, i], v[at, cols], NN)

    def forward():
        places = [
            (b, i, slice(b * BLOCK, (b + 1) * BLOCK), slice(i * DK, (i + 1) * DK))
            for b in range(blocks)
            for i in range(heads)
        ]
        for i in range(heads):
            carried = inc[i]
            for b in range(blocks):
                prior[b, i] = carried.astype(bf16)
                carried = carried + st[b, i]
        for b, i, at, cols in places:
            within[b, i] += dot(q_ref[at, cols], prior[b, i], NN)
        for b, i, at, cols in places:
            mixed, upstream = within[b, i], go_ref[at, cols].astype(f32)
            inverse = 1.0 / jnp.sqrt(jnp.mean(mixed * mixed, axis=-1, keepdims=True) + norm_eps)
            inner = jnp.mean(upstream * mixed, axis=-1, keepdims=True) * inverse
            normed = mixed * inverse
            attn_ref[at, cols] = normed.astype(bf16)
            gm[at, cols] = ((upstream - normed * inner) * inverse).astype(bf16)
        for b, i, at, cols in places:
            gs[b, i] = dot(q_ref[at, cols], gm[at, cols], TN)
        for i in range(heads):
            total = gs[0, i]
            for b in range(1, blocks):
                total = total + gs[b, i]
            loc[i] = total

    def backward_body(b, i, at, cols):
        grad_mixed = gm[at, cols]
        grad_scores = jnp.where(causal, dot(grad_mixed, v[at, cols], NT), 0.0).astype(bf16)
        grad_query = dot(grad_scores, k_ref[at, cols], NN) + dot(grad_mixed, prior[b, i], NT)
        gq_ref[at, cols] = grad_query.astype(bf16)
        gkp[b, i] = dot(grad_scores, q_ref[at, cols], TN)
        gvp[b, i] = dot(sc[b, i], grad_mixed, TN)

    def follow(i):
        carried = inc[i]
        cols = slice(i * DK, (i + 1) * DK)
        for b in reversed(range(blocks)):
            at = slice(b * BLOCK, (b + 1) * BLOCK)
            following16 = carried.astype(bf16)
            following[b, i] = following16
            carried = carried + gs[b, i]
            grad_value = gvp[b, i] + dot(k_ref[at, cols], following16, NN)
            gvt[cols, at] = grad_value.T.astype(bf16)

    for i in range(heads):
        begin_scan(0, i, 0.0)
        later(0.1, within_body, i)
    while tasks:
        earliest = min(tasks)
        tasks.remove(earliest)
        expected = next(earliest[2], None)
        if expected is not None:
            tasks.append((expected, earliest[1], earliest[2]))

    piece = nz * rows
    side = columns // 2

    per_block = feats // piece
    order = []
    for k in (2, 1, 3, 0):
        order += [(dy, k) for dy in (2, 1, 3, 0)] + [(k, dx) for dx in (2, 1, 3, 0)]
    half_side = side // 2
    first, second_half = slice(0, half_side), slice(half_side, side)
    ring = {}

    def hop(which, k, n, forward, source, target):
        axis, position, count = (("seq_0", yy, ny), ("seq_1", xx, nx))[which]
        peer = lax.rem(position + (1 if forward else count - 1), count)
        copy = pltpu.make_async_remote_copy(
            src_ref=source, dst_ref=target,
            send_sem=g1_s.at[which, k, n], recv_sem=g1_r.at[which, k, n],
            device_id={axis: peer}, device_id_type=ID,
        )
        copy.start()
        sent.append(copy)
        ring[which, k, n] = copy

    def begin(which, distance, k, source, target):
        if distance == 2:
            hop(which, k, 0, True, source.at[first], target.at[2, k, first])
            hop(which, k, 1, False, source.at[second_half], target.at[2, k, second_half])
        elif distance == 1:
            hop(which, k, 2, True, source.at[second_half], target.at[0, k, second_half])
        elif distance == 3:
            hop(which, k, 3, False, source.at[first], target.at[1, k, first])

    def pass_on(which, k, ahead, behind, target):
        ring[which, k, 0].wait_recv()
        ahead[first] = (ahead[first].astype(f32) + target[2, k, first].astype(f32)).astype(bf16)
        hop(which, k, 4, True, ahead.at[first], target.at[0, k, first])
        ring[which, k, 1].wait_recv()
        behind[second_half] = (behind[second_half].astype(f32) + target[2, k, second_half].astype(f32)).astype(bf16)
        hop(which, k, 5, False, behind.at[second_half], target.at[1, k, second_half])

    def pass_both(k):
        pass_on(0, k, pa.at[1, k], pa.at[3, k], ra1)
        pass_on(1, k, pb.at[k, 1], pb.at[k, 3], rb1)

    for n, (dy, dx) in enumerate(dict.fromkeys(order)):
        to_y, to_x = lax.rem(yy + dy, ny), lax.rem(xx + dx, nx)
        p = to_y * nx + to_x
        block = p // per_block
        lanes = pl.ds(pl.multiple_of(lax.rem(p, per_block) * piece, piece), piece)
        term = dot(gvt[...], xg[block // 2, lax.rem(block, 2), :, lanes], NN).astype(bf16)
        pa[dy, dx] = term[:side]
        pb[dy, dx] = term[side:]
        begin(0, dy, dx, pa.at[dy, dx], ra1)
        begin(1, dx, dy, pb.at[dy, dx], rb1)
        if n == 11:
            pass_both(2)
    for k in (1, 3, 0):
        pass_both(k)

    def key_body(b, i, at, cols):
        grad_key = gkp[b, i] + dot(v[at, cols], following[b, i], NT)
        gk_ref[at, cols] = grad_key.astype(bf16)

    each_block(key_body)

    def summed_a(dx):
        value = pa[0, dx].astype(f32)
        for n in (2, 3, 4, 5):
            ring[0, dx, n].wait_recv()
        return value + ra1[0, dx].astype(f32) + ra1[1, dx].astype(f32)

    def summed_b(dy):
        value = pb[dy, 0].astype(f32)
        for n in (2, 3, 4, 5):
            ring[1, dy, n].wait_recv()
        return value + rb1[0, dy].astype(f32) + rb1[1, dy].astype(f32)

    def second(axis, position, count, k, source, target, which):
        copy = pltpu.make_async_remote_copy(
            src_ref=source.at[k - 1], dst_ref=target.at[k - 1],
            send_sem=g_s.at[which, k - 1], recv_sem=g_r.at[which, k - 1],
            device_id={axis: lax.rem(position + k, count)}, device_id_type=ID,
        )
        copy.start()
        sent.append(copy)
        return copy

    a2, b2 = [], []
    for k in (2, 1, 3):
        if k < nx:
            sa2[k - 1] = summed_a(k).astype(bf16)
            a2.append(second("seq_1", xx, nx, k, sa2, ra2, 0))
        if k < ny:
            sb2[k - 1] = summed_b(k).astype(bf16)
            b2.append(second("seq_0", yy, ny, k, sb2, rb2, 1))
    final_a, final_b = summed_a(0), summed_b(0)

    def last(final, second_copies, received, which):
        for copy in second_copies:
            copy.wait_recv()
        for kk in range(len(second_copies)):
            final += received[kk].astype(f32)
        final = final.T
        tzf[which] = final
        tz[which] = final.astype(bf16)
        return exchange(
            "seq_2", nz, lambda p: tz.at[which, pl.ds(pl.multiple_of(p * rows, rows), rows)],
            lambda kk: rz.at[which, kk - 1], g_s.at[2 + which], g_r.at[2 + which],
        )

    z3 = [last(final_a, a2, ra2, 0), last(final_b, b2, rb2, 1)]
    for which, copies in enumerate(z3):
        sent += copies
        result = tzf[which, pl.ds(pl.multiple_of(zh * rows, rows), rows)]
        arrive(copies)
        for kk in range(nz - 1):
            result += rz[which, kk].astype(f32)
        gl_ref[:, which * side : (which + 1) * side] = result

    for copy in sent:
        copy.wait_send()

    @pl.loop(0, nl)
    def _(block):
        @pl.loop(0, CHUNKS)
        def _(j):
            side_copy(block, j).wait_send()

            @pl.when(jnp.logical_and(block <= zl, zl < nl - 1))
            def _():
                line_copy(block, j, True).wait_send()

            @pl.when(jnp.logical_and(block >= zl, zl > 0))
            def _():
                line_copy(block, j, False).wait_send()


def deliver(*refs):
    copies = [pltpu.make_async_copy(refs[i], refs[4 + i], refs[8].at[i]) for i in range(4)]
    for copy in copies:
        copy.start()
    for copy in copies:
        copy.wait()


def per_device(inputs, latent, queries, keys, grad_out):
    sizes = tuple(lax.axis_size(a) for a in (*SEQ, "head_0"))
    ny, nx, nz, nl = sizes
    tokens, feats = inputs.shape
    rows, columns = latent.shape
    heads, blocks = columns // DK, tokens // BLOCK
    seqs, everyone = ny * nx * nz, ny * nx * nz * rows
    side, piece = columns // 2, nz * rows
    dma = pltpu.SemaphoreType.DMA
    most = max(ny, nx, nz) - 1
    scratch = [
        pltpu.VMEM(latent.shape, f32),
        pltpu.VMEM((tokens, columns), bf16),
        pltpu.VMEM((tokens, columns), bf16),
        pltpu.VMEM((tokens, columns), bf16),
        pltpu.VMEM((seqs, rows // 2, columns), bf16),
        pltpu.VMEM((seqs, rows // 2, columns), bf16),
        pltpu.VMEM((everyone, columns), bf16),
        pltpu.VMEM((nl, 2, tokens, feats), bf16),
        pltpu.VMEM((tokens, columns), f32),
        pltpu.VMEM((tokens, columns), bf16),
        pltpu.VMEM((blocks, heads, BLOCK, BLOCK), bf16),
        pltpu.VMEM((blocks, heads, DK, DK), f32),
        pltpu.VMEM((blocks, heads, DK, DK), bf16),
        pltpu.VMEM((blocks, heads, BLOCK, DK), f32),
        pltpu.VMEM((tokens, columns), bf16),
        pltpu.VMEM((blocks, heads, DK, DK), f32),
        pltpu.VMEM((blocks, heads, DK, DK), bf16),
        pltpu.VMEM((blocks, heads, BLOCK, DK), f32),
        pltpu.VMEM((blocks, heads, BLOCK, DK), f32),
        pltpu.VMEM((columns, tokens), bf16),
        pltpu.VMEM((heads, DK, DK), f32),
        pltpu.VMEM((2, heads, 2, 4, DK // 2, DK), bf16),
        pltpu.VMEM((2, heads, 2, 2, most, DK // 2, DK), bf16),
        pltpu.VMEM((2, heads, 2, 3, DK // 2, DK), bf16),
        pltpu.VMEM((heads, DK, DK), f32),
        pltpu.VMEM((ny, nx, side, piece), bf16),
        pltpu.VMEM((ny, nx, side, piece), bf16),
        pltpu.VMEM((ny - 1, nx, side, piece), bf16),
        pltpu.VMEM((nx - 1, ny, side, piece), bf16),
        pltpu.VMEM((nx - 1, side, piece), bf16),
        pltpu.VMEM((ny - 1, side, piece), bf16),
        pltpu.VMEM((nx - 1, side, piece), bf16),
        pltpu.VMEM((ny - 1, side, piece), bf16),
        pltpu.VMEM((2, piece, side), bf16),
        pltpu.VMEM((2, piece, side), f32),
        pltpu.VMEM((2, nz - 1, rows, side), bf16),
        dma((5,)),
        dma((6,)), dma((6,)),
        dma((2, most)), dma((2, most)),
        dma((2, most)), dma((2, most)),
        dma((nl, CHUNKS)), dma((nl, CHUNKS)), dma((nl, CHUNKS)),
        dma((nl, CHUNKS)), dma((nl, CHUNKS)),
        dma((2, heads, 2, 2, most)), dma((2, heads, 2, 2, most)),
        dma((2, heads, 2, 3)), dma((2, heads, 2, 3)),
        dma((2, 4, 6)), dma((2, 4, 6)),
        dma((4, most)), dma((4, most)),
    ]
    like = jax.ShapeDtypeStruct(queries.shape, bf16)
    results = pl.pallas_call(
        functools.partial(kernel, sizes),
        out_shape=(like, like, like, jax.ShapeDtypeStruct(latent.shape, f32)),
        in_specs=[pl.BlockSpec(memory_space=pltpu.HBM)] * 5,
        out_specs=(pl.BlockSpec(memory_space=pltpu.VMEM),) * 4,
        scratch_shapes=scratch,
        compiler_params=pltpu.CompilerParams(
            collective_id=0, has_side_effects=True, vmem_limit_bytes=40 << 20
        ),
    )(*(pltpu.with_memory_space_constraint(a, pltpu.HBM) for a in (inputs, latent, queries, keys, grad_out)))
    return pl.pallas_call(
        deliver,
        out_shape=(like, like, like, jax.ShapeDtypeStruct(latent.shape, f32)),
        in_specs=[pl.BlockSpec(memory_space=pltpu.VMEM)] * 4,
        out_specs=(pl.BlockSpec(memory_space=pltpu.HBM),) * 4,
        scratch_shapes=[pltpu.SemaphoreType.DMA((4,))],
        compiler_params=pltpu.CompilerParams(vmem_limit_bytes=4 << 20),
    )(*results)


def solution(mesh):
    torus = Mesh(mesh.devices.reshape(4, 4, 4, 4, 2), (*SEQ, *HEAD))
    placed = P(SEQ, HEAD)
    return jax.shard_map(
        per_device,
        mesh=torus,
        in_specs=(placed,) * 5,
        out_specs=(placed,) * 4,
        check_vma=False,
    )
```

```python
import functools
import itertools

import jax
import jax.numpy as jnp
from jax import lax
from jax.experimental import pallas as pl
from jax.experimental.pallas import tpu as pltpu
from jax.sharding import Mesh
from jax.sharding import PartitionSpec as P

DK = 128
BLOCK = 128
HEAD = ("head_0", "head_1")
SEQ = ("seq_0", "seq_1", "seq_2")
ID = pl.DeviceIdType.MESH
CHUNKS = 4
EARLY = 2

absmean_eps = 1e-05
norm_eps = 1e-06

f32 = jnp.float32
bf16 = jnp.bfloat16


def dot(a, b, contract):
    return lax.dot_general(a, b, ((contract[:1], contract[1:]), ((), ())), preferred_element_type=f32)


NN, NT, TN = (1, 0), (1, 1), (0, 0)


def exchange(axis, count, source, target, send, recv, shared=False):
    position = lax.axis_index(axis)
    copies = {}
    for kk in sorted(range(1, count), key=lambda kk: abs(2 * kk - count)):
        peer = lax.rem(position + kk, count)
        copy = pltpu.make_async_remote_copy(
            src_ref=source(peer),
            dst_ref=target(kk),
            send_sem=send if shared else send.at[kk - 1],
            recv_sem=recv.at[kk - 1],
            device_id={axis: peer},
            device_id_type=ID,
        )
        copy.start()
        copies[kk] = copy
    return [copies[kk] for kk in range(1, count)]


def arrive(copies):
    for copy in copies:
        copy.wait_recv()


def kernel(
    sizes, x_in, latent_in, q_in, k_in, go_in, attn_ref, gq_ref, gk_ref, gl_ref,
    latent_ref, q_ref, k_ref, go_ref, wa, wb, wt, xg, acc, v, sc, st, prior, within, gm, gs, following, gkp, gvp, gvt, loc, scan_send, scan_recv, zr, inc,
    pa, pb, ra1, rb1, sa2, sb2, ra2, rb2, tz, tzf, rz,
    own_sem, wz_s, wz_r, w2_s, w2_r, w3_s, w3_r, xp_s, xm_s, xs_s, xl_r, xs_r, scan_s, scan_r, zs_s, zs_r, g1_s, g1_r, g_s, g_r,
):
    ny, nx, nz, nl = sizes
    yy, xx, zh = (lax.axis_index(a) for a in SEQ)
    zl, cc = (lax.axis_index(a) for a in HEAD)
    tokens, feats = x_in.shape
    rows, columns = latent_ref.shape
    half = rows // 2
    heads = columns // DK
    blocks = tokens // BLOCK
    step = tokens // CHUNKS
    sent, left = [], []

    fetches = [
        pltpu.make_async_copy(latent_in, latent_ref, own_sem.at[0]),
        pltpu.make_async_copy(x_in, xg.at[zl, cc], own_sem.at[1]),
        pltpu.make_async_copy(q_in, q_ref, own_sem.at[2]),
        pltpu.make_async_copy(k_in, k_ref, own_sem.at[3]),
        pltpu.make_async_copy(go_in, go_ref, own_sem.at[4]),
    ]
    for fetch in fetches:
        fetch.start()
    at_a = (yy * nx + xx) * nz
    at_b = (xx * ny + yy) * nz
    barrier = pltpu.get_barrier_semaphore()
    for axis, count in (("seq_2", nz), ("seq_1", nx), ("seq_0", ny), ("head_1", 2)):
        position = lax.axis_index(axis)
        for kk in range(1, count):
            pl.semaphore_signal(
                barrier, inc=1, device_id={axis: lax.rem(position + kk, count)}, device_id_type=ID
            )

    @pl.when(zl > 0)
    def _():
        pl.semaphore_signal(barrier, inc=1, device_id={"head_0": zl - 1}, device_id_type=ID)

    @pl.when(zl < nl - 1)
    def _():
        pl.semaphore_signal(barrier, inc=1, device_id={"head_0": zl + 1}, device_id_type=ID)

    fetches[0].wait()
    latent16 = latent_ref[...].astype(bf16)
    wa[at_a + zh] = latent16[:half]
    wb[at_b + zh] = latent16[half:]
    fetches[1].wait()
    partners = (nz - 1) + (nx - 1) + (ny - 1) + 1
    neighbours = jnp.where(zl > 0, 1, 0) + jnp.where(zl < nl - 1, 1, 0)
    pl.semaphore_wait(barrier, partners + neighbours)

    up, down = lax.rem(zh + 1, nz), lax.rem(zh + nz - 1, nz)
    opposite = lax.rem(zh + 2, nz)

    def z_copy(peer, source, target, send, recv, alone=True):
        copy = pltpu.make_async_remote_copy(
            src_ref=source, dst_ref=target, send_sem=send, recv_sem=recv,
            device_id={"seq_2": peer}, device_id_type=ID,
        )
        copy.start()
        if alone:
            sent.append(copy)
        return copy

    def w_copy(peer, ref, at, n):
        return z_copy(peer, ref.at[at], ref.at[at], wz_s.at[n], wz_r.at[n])

    wz = [
        w_copy(up, wa, at_a + zh, 0),
        w_copy(down, wb, at_b + zh, 1),
        w_copy(up, wb, at_b + zh, 2),
        w_copy(down, wa, at_a + zh, 3),
    ]

    def rows_of(ref, j):
        return ref.at[pl.ds(pl.multiple_of(j * step, step), step)]

    def line_copy(block, j, up):
        place = rows_of(xg.at[block, cc], j)
        return pltpu.make_async_remote_copy(
            src_ref=place,
            dst_ref=place,
            send_sem=(xp_s if up else xm_s).at[block],
            recv_sem=xl_r.at[block, j],
            device_id={"head_0": zl + 1 if up else zl - 1},
            device_id_type=ID,
        )

    def side_copy(block, j):
        place = rows_of(xg.at[block, cc], j)
        return pltpu.make_async_remote_copy(
            src_ref=place,
            dst_ref=place,
            send_sem=xs_s.at[block],
            recv_sem=xs_r.at[block, j],
            device_id={"head_1": 1 - cc},
            device_id_type=ID,
        )

    def send_own(first, last):
        @pl.loop(first, last)
        def _(j):
            @pl.when(zl < nl - 1)
            def _():
                line_copy(zl, j, True).start()

            @pl.when(zl > 0)
            def _():
                line_copy(zl, j, False).start()

            side_copy(zl, j).start()

    send_own(0, EARLY)

    def relay(distance, first, last):
        @pl.loop(first, last)
        def _(j):
            @pl.when(zl >= distance)
            def _():
                block = zl - distance
                line_copy(block, j, True).wait_recv()

                @pl.when(zl < nl - 1)
                def _():
                    line_copy(block, j, True).start()

                side_copy(block, j).start()

            @pl.when(zl + distance < nl)
            def _():
                block = zl + distance
                line_copy(block, j, False).wait_recv()

                @pl.when(zl > 0)
                def _():
                    line_copy(block, j, False).start()

                side_copy(block, j).start()

    causal = lax.broadcasted_iota(jnp.int32, (BLOCK, BLOCK), 0) >= lax.broadcasted_iota(
        jnp.int32, (BLOCK, BLOCK), 1
    )

    def unrolled(body, first, last):
        for b in range(first, last):
            for i in range(heads):
                body(b, i, slice(b * BLOCK, (b + 1) * BLOCK), slice(i * DK, (i + 1) * DK))

    def each_block(body):
        @pl.loop(0, blocks)
        def _(b):
            at = pl.ds(pl.multiple_of(b * BLOCK, BLOCK), BLOCK)
            for i in range(heads):
                body(b, i, at, slice(i * DK, (i + 1) * DK))

    def scores_body(b, i, at, cols):
        s = dot(q_ref[at, cols], k_ref[at, cols], NT)
        sc[b, i] = jnp.where(causal, s, 0.0).astype(bf16)

    for fetch in fetches[2:]:
        fetch.wait()
    each_block(scores_body)

    wz[0].wait_recv()
    wz += [w_copy(up, wa, at_a + down, 4)]
    wz[1].wait_recv()
    wz += [w_copy(down, wb, at_b + up, 5)]
    send_own(EARLY, CHUNKS)
    relay(1, 0, CHUNKS // 2)
    arrive(wz[2:])
    mine_a = wa.at[pl.ds(at_a, nz)]
    mine_b = wb.at[pl.ds(at_b, nz)]
    w2a = exchange("seq_1", nx, lambda p: mine_a, lambda kk: mine_a, w2_s.at[0], w2_r.at[0])
    w2b = exchange("seq_0", ny, lambda p: mine_b, lambda kk: mine_b, w2_s.at[1], w2_r.at[1])
    sent += w2a + w2b
    relay(1, CHUNKS // 2, CHUNKS)
    row_a = wa.at[pl.ds(yy * nx * nz, nx * nz)]
    row_b = wb.at[pl.ds(xx * ny * nz, ny * nz)]
    arrive(w2a)
    w3a = exchange("seq_0", ny, lambda p: row_a, lambda kk: row_a, w3_s.at[0], w3_r.at[0])
    arrive(w2b)
    w3b = exchange("seq_1", nx, lambda p: row_b, lambda kk: row_b, w3_s.at[1], w3_r.at[1])
    sent += w3a + w3b
    for distance in range(2, nl - 1):
        relay(distance, 0, CHUNKS)
    arrive(w3a)
    arrive(w3b)
    far = nl - 1 - zl

    def at_end(body):
        pl.when(jnp.logical_or(zl == 0, zl == nl - 1))(body)

    def share_far(first, last):
        @at_end
        def _():
            @pl.loop(first, last)
            def _(j):
                line_copy(far, j, True).wait_recv()
                side_copy(far, j).start()

    share_far(0, 1)

    def magnitude(s, total):
        both = jnp.abs(wa[s].astype(f32)) + jnp.abs(wb[s].astype(f32))
        return total + both.reshape(half // 8, 8, columns).sum(axis=0)

    total = lax.fori_loop(0, ny * nx * nz, magnitude, jnp.zeros((8, columns), f32))
    scale = total.sum(axis=0, keepdims=True) / (ny * nx * nz * rows) + absmean_eps
    halfway = 0.5 * scale

    def ternary(w):
        w = w.astype(f32)
        return jnp.where(w > halfway, scale, jnp.where(w < -halfway, -scale, 0.0)).astype(bf16)

    @pl.loop(0, ny * nx)
    def _(p):
        other = lax.rem(p, nx) * ny + p // nx
        for z in range(nz):
            at = pl.multiple_of((p * nz + z) * rows, rows)
            wt[pl.ds(at, half)] = ternary(wa[p * nz + z])
            wt[pl.ds(pl.multiple_of(at + half, half), half)] = ternary(wb[other * nz + z])

    share_far(1, 2)
    acc[...] = jnp.zeros_like(acc)

    def features(block, core):
        return wt[pl.ds(pl.multiple_of((block * 2 + core) * feats, feats), feats)]

    @pl.loop(0, nl)
    def _(block):
        @pl.when(jnp.abs(block - zl) < nl - 1)
        def _():
            @pl.loop(0, CHUNKS)
            def _(j):
                side_copy(block, j).wait_recv()

            @pl.loop(0, 2)
            def _(core):
                acc[...] += dot(xg[block, core], features(block, core), NN)

    share_far(2, CHUNKS // 2 + 1)

    @at_end
    def _():
        half_at = pl.ds(0, tokens // 2)

        @pl.loop(0, CHUNKS // 2)
        def _(j):
            side_copy(far, j).wait_recv()

        acc[half_at] += dot(xg[far, cc, half_at], features(far, cc), NN)
        acc[half_at] += dot(xg[far, 1 - cc, half_at], features(far, 1 - cc), NN)

        def multiply(core, j):
            at = slice(j * step, (j + 1) * step)
            acc[at] += dot(xg[far, core, at], features(far, core), NN)

        for j in range(CHUNKS // 2, CHUNKS):
            if j > CHUNKS // 2:
                line_copy(far, j, True).wait_recv()
                side_copy(far, j).start()
                side_copy(far, j - 1).wait_recv()
                multiply(1 - cc, j - 1)
            multiply(cc, j)
        side_copy(far, CHUNKS - 1).wait_recv()
        multiply(1 - cc, CHUNKS - 1)

    def all_left(ref, semaphore):
        pltpu.make_async_remote_copy(
            src_ref=ref, dst_ref=ref, send_sem=semaphore, recv_sem=semaphore,
            device_id={"head_1": 1 - cc}, device_id_type=ID,
        ).wait_send()

    @pl.when(zl == nl - 2)
    def _():
        all_left(xg.at[0, cc], xp_s.at[0])

    @pl.when(zl == 1)
    def _():
        all_left(xg.at[nl - 1, cc], xm_s.at[nl - 1])

    v[...] = acc[...].astype(bf16)

    totals = [jnp.zeros((DK, DK), f32)] * heads

    def state_body(b, i, at, cols):
        s = dot(k_ref[at, cols], v[at, cols], TN)
        st[b, i] = s
        totals[i] = totals[i] + s

    unrolled(state_body, 0, blocks)
    for i in range(heads):
        loc[i] = totals[i]

    part = DK // 2
    tasks, serial = [], itertools.count()
    finished = {}

    def exchange_part(axis, count, which, i, r, stage, slot):
        copies = exchange(
            axis, count, lambda p: scan_send.at[which, i, r, slot], lambda kk: scan_recv.at[which, i, r, stage, kk - 1],
            scan_s.at[which, i, r, stage], scan_r.at[which, i, r, stage], True,
        )
        left.append((scan_send.at[which, i, r, 0 : count - 1], scan_s.at[which, i, r, stage]))
        return copies

    def collect(axis, count, which, i, r, stage, copies, mine):
        position = lax.axis_index(axis)
        before, everything = jnp.zeros((part, DK), f32), mine
        for kk in range(1, count):
            copies[kk - 1].wait_recv()
            value = scan_recv[which, i, r, stage, kk - 1].astype(f32)
            sender = lax.rem(position + count - kk, count)
            before += jnp.where(earlier(which, sender, position), value, 0.0)
            everything += value
        return before, everything

    def earlier(which, p, mine):
        return p > mine if which else p < mine

    def step_z(which, i, r, n, peer, source, target):
        if n == 0:
            left.append((scan_send.at[which, i, r, 0 : nz - 1], zs_s.at[which, i, r]))
        return z_copy(peer, source, target, zs_s.at[which, i, r], zs_r.at[which, i, r, n], False)

    def chain_xyz(which, i, r, now):
        send, arrived = scan_send.at[which, i, r], zr.at[which, i, r]
        own = slice(r * part, (r + 1) * part)
        value = loc[i, own]
        send[0] = value.astype(bf16)
        copies = exchange_part("seq_1", nx, which, i, r, 0, 0)
        yield now + 3.3
        before, row = collect("seq_1", nx, which, i, r, 0, copies, value)
        send[1] = row.astype(bf16)
        copies = exchange_part("seq_0", ny, which, i, r, 1, 1)
        yield now + 6.4
        more, _ = collect("seq_0", ny, which, i, r, 1, copies, row)
        before += more
        send[2] = before.astype(bf16)
        send[3] = (before + loc[i, own]).astype(bf16)

        def message(peer):
            return send.at[2 + jnp.where(earlier(which, zh, peer), 1, 0)]

        az = [
            step_z(which, i, r, n, peer, message(peer), arrived.at[n])
            for n, peer in ((0, opposite), (1, up), (2, down))
        ]
        yield now + 14.4
        arrive(az)
        inc[i, own] = before + arrived[0].astype(f32) + arrived[1].astype(f32) + arrived[2].astype(f32)
        done(which, now + 14.4)

    def chain_zxy(which, i, r, now):
        send, arrived = scan_send.at[which, i, r], zr.at[which, i, r]
        own = slice(r * part, (r + 1) * part)
        send[0] = loc[i, own].astype(bf16)
        bz = [
            step_z(which, i, r, n, peer, send.at[0], arrived.at[n])
            for n, peer in ((0, opposite), (1, up), (2, down))
        ]
        yield now + 8.0
        before, line = jnp.zeros((part, DK), f32), loc[i, own]
        for n, sender in ((0, opposite), (1, down), (2, up)):
            bz[n].wait_recv()
            value = arrived[n].astype(f32)
            before += jnp.where(earlier(which, sender, zh), value, 0.0)
            line += value
        send[1] = line.astype(bf16)
        copies = exchange_part("seq_1", nx, which, i, r, 0, 1)
        yield now + 11.3
        more, plane = collect("seq_1", nx, which, i, r, 0, copies, line)
        before += more
        send[2] = plane.astype(bf16)
        copies = exchange_part("seq_0", ny, which, i, r, 1, 2)
        yield now + 14.6
        more, _ = collect("seq_0", ny, which, i, r, 1, copies, plane)
        inc[i, own] = before + more
        done(which, now + 14.6)

    def begin_scan(which, i, now):
        for r in range(2):
            chain = chain_zxy if i % 2 else chain_xyz
            tasks.append((now + 0.01 * r, next(serial), chain(which, i, r, now + 0.5 * r)))

    def work(body, i, first, last):
        for b in range(first, last):
            body(b, i, slice(b * BLOCK, (b + 1) * BLOCK), slice(i * DK, (i + 1) * DK))
        return
        yield

    def later(now, body, i):
        for t in range(2):
            tasks.append((now + 0.7 * t, next(serial), work(body, i, blocks // 2 * t, blocks // 2 * (t + 1))))

    def done(which, now):
        finished[which] = finished.get(which, 0) + 1
        if finished[which] < 2 * heads:
            return
        if which:
            for i in range(heads):
                follow(i)
            return
        forward()
        for i in reversed(range(heads)):
            begin_scan(1, i, now + 2.0)
        for i in range(heads):
            later(now + 2.1, backward_body, i)

    def within_body(b, i, at, cols):
        within[b, i] = dot(sc[b, i], v[at, cols], NN)

    def forward():
        places = [
            (b, i, slice(b * BLOCK, (b + 1) * BLOCK), slice(i * DK, (i + 1) * DK))
            for b in range(blocks)
            for i in range(heads)
        ]
        for i in range(heads):
            carried = inc[i]
            for b in range(blocks):
                prior[b, i] = carried.astype(bf16)
                carried = carried + st[b, i]
        for b, i, at, cols in places:
            within[b, i] += dot(q_ref[at, cols], prior[b, i], NN)
        for b, i, at, cols in places:
            mixed, upstream = within[b, i], go_ref[at, cols].astype(f32)
            inverse = 1.0 / jnp.sqrt(jnp.mean(mixed * mixed, axis=-1, keepdims=True) + norm_eps)
            inner = jnp.mean(upstream * mixed, axis=-1, keepdims=True) * inverse
            normed = mixed * inverse
            attn_ref[at, cols] = normed.astype(bf16)
            gm[at, cols] = ((upstream - normed * inner) * inverse).astype(bf16)
        for b, i, at, cols in places:
            gs[b, i] = dot(q_ref[at, cols], gm[at, cols], TN)
        for i in range(heads):
            total = gs[0, i]
            for b in range(1, blocks):
                total = total + gs[b, i]
            loc[i] = total

    def backward_body(b, i, at, cols):
        grad_mixed = gm[at, cols]
        grad_scores = jnp.where(causal, dot(grad_mixed, v[at, cols], NT), 0.0).astype(bf16)
        grad_query = dot(grad_scores, k_ref[at, cols], NN) + dot(grad_mixed, prior[b, i], NT)
        gq_ref[at, cols] = grad_query.astype(bf16)
        gkp[b, i] = dot(grad_scores, q_ref[at, cols], TN)
        gvp[b, i] = dot(sc[b, i], grad_mixed, TN)

    def follow(i):
        carried = inc[i]
        cols = slice(i * DK, (i + 1) * DK)
        for b in reversed(range(blocks)):
            at = slice(b * BLOCK, (b + 1) * BLOCK)
            following16 = carried.astype(bf16)
            following[b, i] = following16
            carried = carried + gs[b, i]
            grad_value = gvp[b, i] + dot(k_ref[at, cols], following16, NN)
            gvt[cols, at] = grad_value.T.astype(bf16)

    for i in range(heads):
        begin_scan(0, i, 0.0)
        later(0.1, within_body, i)
    while tasks:
        earliest = min(tasks)
        tasks.remove(earliest)
        expected = next(earliest[2], None)
        if expected is not None:
            tasks.append((expected, earliest[1], earliest[2]))

    piece = nz * rows
    side = columns // 2

    per_block = feats // piece
    order = []
    for k in (2, 1, 3, 0):
        order += [(dy, k) for dy in (2, 1, 3, 0)] + [(k, dx) for dx in (2, 1, 3, 0)]
    half_side = side // 2
    first, second_half = slice(0, half_side), slice(half_side, side)
    ring = {}

    def hop(which, k, n, forward, source, target):
        axis, position, count = (("seq_0", yy, ny), ("seq_1", xx, nx))[which]
        peer = lax.rem(position + (1 if forward else count - 1), count)
        copy = pltpu.make_async_remote_copy(
            src_ref=source, dst_ref=target,
            send_sem=g1_s.at[which, k], recv_sem=g1_r.at[which, k, n],
            device_id={axis: peer}, device_id_type=ID,
        )
        copy.start()
        ring[which, k, n] = copy

    def begin(which, distance, k, source, target):
        if distance == 2:
            hop(which, k, 0, True, source.at[first], target.at[2, k, first])
            hop(which, k, 1, False, source.at[second_half], target.at[2, k, second_half])
        elif distance == 1:
            hop(which, k, 2, True, source.at[second_half], target.at[0, k, second_half])
        elif distance == 3:
            hop(which, k, 3, False, source.at[first], target.at[1, k, first])

    def pass_on(which, k, ahead, behind, target):
        ring[which, k, 0].wait_recv()
        ahead[first] = (ahead[first].astype(f32) + target[2, k, first].astype(f32)).astype(bf16)
        hop(which, k, 4, True, ahead.at[first], target.at[0, k, first])
        ring[which, k, 1].wait_recv()
        behind[second_half] = (behind[second_half].astype(f32) + target[2, k, second_half].astype(f32)).astype(bf16)
        hop(which, k, 5, False, behind.at[second_half], target.at[1, k, second_half])

    def pass_both(k):
        pass_on(0, k, pa.at[1, k], pa.at[3, k], ra1)
        pass_on(1, k, pb.at[k, 1], pb.at[k, 3], rb1)

    for n, (dy, dx) in enumerate(dict.fromkeys(order)):
        to_y, to_x = lax.rem(yy + dy, ny), lax.rem(xx + dx, nx)
        p = to_y * nx + to_x
        block = p // per_block
        lanes = pl.ds(pl.multiple_of(lax.rem(p, per_block) * piece, piece), piece)
        term = dot(gvt[...], xg[block // 2, lax.rem(block, 2), :, lanes], NN).astype(bf16)
        pa[dy, dx] = term[:side]
        pb[dy, dx] = term[side:]
        begin(0, dy, dx, pa.at[dy, dx], ra1)
        begin(1, dx, dy, pb.at[dy, dx], rb1)
        if n == 11:
            pass_both(2)
    left += [(ref.at[0:3, 0], g1_s.at[which, k]) for which, ref in ((0, pa), (1, pb)) for k in range(4)]

    def summed_a(dx):
        value = pa[0, dx].astype(f32)
        for n in (2, 3, 4, 5):
            ring[0, dx, n].wait_recv()
        return value + ra1[0, dx].astype(f32) + ra1[1, dx].astype(f32)

    def summed_b(dy):
        value = pb[dy, 0].astype(f32)
        for n in (2, 3, 4, 5):
            ring[1, dy, n].wait_recv()
        return value + rb1[0, dy].astype(f32) + rb1[1, dy].astype(f32)

    def second(axis, position, count, k, source, target, which):
        copy = pltpu.make_async_remote_copy(
            src_ref=source.at[k - 1], dst_ref=target.at[k - 1],
            send_sem=g_s.at[which, k - 1], recv_sem=g_r.at[which, k - 1],
            device_id={axis: lax.rem(position + k, count)}, device_id_type=ID,
        )
        copy.start()
        sent.append(copy)
        return copy

    a2, b2 = [], []

    def second_both(k):
        sa2[k - 1] = summed_a(k).astype(bf16)
        a2.append(second("seq_1", xx, nx, k, sa2, ra2, 0))
        sb2[k - 1] = summed_b(k).astype(bf16)
        b2.append(second("seq_0", yy, ny, k, sb2, rb2, 1))

    pass_both(1)
    second_both(2)
    pass_both(3)
    second_both(1)
    pass_both(0)
    second_both(3)

    def key_body(b, i, at, cols):
        grad_key = gkp[b, i] + dot(v[at, cols], following[b, i], NT)
        gk_ref[at, cols] = grad_key.astype(bf16)

    each_block(key_body)

    final_a, final_b = summed_a(0), summed_b(0)

    def last(final, second_copies, received, which):
        for copy in second_copies:
            copy.wait_recv()
        for kk in range(len(second_copies)):
            final += received[kk].astype(f32)
        final = final.T
        tzf[which] = final
        tz[which] = final.astype(bf16)
        return exchange(
            "seq_2", nz, lambda p: tz.at[which, pl.ds(pl.multiple_of(p * rows, rows), rows)],
            lambda kk: rz.at[which, kk - 1], g_s.at[2 + which], g_r.at[2 + which],
        )

    z3 = [last(final_a, a2, ra2, 0), last(final_b, b2, rb2, 1)]
    for which, copies in enumerate(z3):
        sent += copies
        result = tzf[which, pl.ds(pl.multiple_of(zh * rows, rows), rows)]
        arrive(copies)
        for kk in range(nz - 1):
            result += rz[which, kk].astype(f32)
        gl_ref[:, which * side : (which + 1) * side] = result

    for copy in sent:
        copy.wait_send()

    for ref, semaphore in left:
        all_left(ref, semaphore)

    @pl.loop(0, nl)
    def _(block):
        place = xg.at[block, cc]
        all_left(place, xs_s.at[block])
        ahead = jnp.logical_and(zl == nl - 2, block == 0)
        behind = jnp.logical_and(zl == 1, block == nl - 1)

        @pl.when(jnp.logical_and(jnp.logical_and(block <= zl, zl < nl - 1), jnp.logical_not(ahead)))
        def _():
            all_left(place, xp_s.at[block])

        @pl.when(jnp.logical_and(jnp.logical_and(block >= zl, zl > 0), jnp.logical_not(behind)))
        def _():
            all_left(place, xm_s.at[block])


def deliver(*refs):
    copies = [pltpu.make_async_copy(refs[i], refs[4 + i], refs[8].at[i]) for i in range(4)]
    for copy in copies:
        copy.start()
    for copy in copies:
        copy.wait()


def per_device(inputs, latent, queries, keys, grad_out):
    sizes = tuple(lax.axis_size(a) for a in (*SEQ, "head_0"))
    ny, nx, nz, nl = sizes
    tokens, feats = inputs.shape
    rows, columns = latent.shape
    heads, blocks = columns // DK, tokens // BLOCK
    seqs, everyone = ny * nx * nz, ny * nx * nz * rows
    side, piece = columns // 2, nz * rows
    dma = pltpu.SemaphoreType.DMA
    most = max(ny, nx, nz) - 1
    scratch = [
        pltpu.VMEM(latent.shape, f32),
        pltpu.VMEM((tokens, columns), bf16),
        pltpu.VMEM((tokens, columns), bf16),
        pltpu.VMEM((tokens, columns), bf16),
        pltpu.VMEM((seqs, rows // 2, columns), bf16),
        pltpu.VMEM((seqs, rows // 2, columns), bf16),
        pltpu.VMEM((everyone, columns), bf16),
        pltpu.VMEM((nl, 2, tokens, feats), bf16),
        pltpu.VMEM((tokens, columns), f32),
        pltpu.VMEM((tokens, columns), bf16),
        pltpu.VMEM((blocks, heads, BLOCK, BLOCK), bf16),
        pltpu.VMEM((blocks, heads, DK, DK), f32),
        pltpu.VMEM((blocks, heads, DK, DK), bf16),
        pltpu.VMEM((blocks, heads, BLOCK, DK), f32),
        pltpu.VMEM((tokens, columns), bf16),
        pltpu.VMEM((blocks, heads, DK, DK), f32),
        pltpu.VMEM((blocks, heads, DK, DK), bf16),
        pltpu.VMEM((blocks, heads, BLOCK, DK), f32),
        pltpu.VMEM((blocks, heads, BLOCK, DK), f32),
        pltpu.VMEM((columns, tokens), bf16),
        pltpu.VMEM((heads, DK, DK), f32),
        pltpu.VMEM((2, heads, 2, 4, DK // 2, DK), bf16),
        pltpu.VMEM((2, heads, 2, 2, most, DK // 2, DK), bf16),
        pltpu.VMEM((2, heads, 2, 3, DK // 2, DK), bf16),
        pltpu.VMEM((heads, DK, DK), f32),
        pltpu.VMEM((ny, nx, side, piece), bf16),
        pltpu.VMEM((ny, nx, side, piece), bf16),
        pltpu.VMEM((ny - 1, nx, side, piece), bf16),
        pltpu.VMEM((nx - 1, ny, side, piece), bf16),
        pltpu.VMEM((nx - 1, side, piece), bf16),
        pltpu.VMEM((ny - 1, side, piece), bf16),
        pltpu.VMEM((nx - 1, side, piece), bf16),
        pltpu.VMEM((ny - 1, side, piece), bf16),
        pltpu.VMEM((2, piece, side), bf16),
        pltpu.VMEM((2, piece, side), f32),
        pltpu.VMEM((2, nz - 1, rows, side), bf16),
        dma((5,)),
        dma((6,)), dma((6,)),
        dma((2, most)), dma((2, most)),
        dma((2, most)), dma((2, most)),
        dma((nl,)), dma((nl,)), dma((nl,)),
        dma((nl, CHUNKS)), dma((nl, CHUNKS)),
        dma((2, heads, 2, 2)), dma((2, heads, 2, 2, most)),
        dma((2, heads, 2)), dma((2, heads, 2, 3)),
        dma((2, 4)), dma((2, 4, 6)),
        dma((4, most)), dma((4, most)),
    ]
    like = jax.ShapeDtypeStruct(queries.shape, bf16)
    results = pl.pallas_call(
        functools.partial(kernel, sizes),
        out_shape=(like, like, like, jax.ShapeDtypeStruct(latent.shape, f32)),
        in_specs=[pl.BlockSpec(memory_space=pltpu.HBM)] * 5,
        out_specs=(pl.BlockSpec(memory_space=pltpu.VMEM),) * 4,
        scratch_shapes=scratch,
        compiler_params=pltpu.CompilerParams(
            collective_id=0, has_side_effects=True, vmem_limit_bytes=40 << 20
        ),
    )(*(pltpu.with_memory_space_constraint(a, pltpu.HBM) for a in (inputs, latent, queries, keys, grad_out)))
    return pl.pallas_call(
        deliver,
        out_shape=(like, like, like, jax.ShapeDtypeStruct(latent.shape, f32)),
        in_specs=[pl.BlockSpec(memory_space=pltpu.VMEM)] * 4,
        out_specs=(pl.BlockSpec(memory_space=pltpu.HBM),) * 4,
        scratch_shapes=[pltpu.SemaphoreType.DMA((4,))],
        compiler_params=pltpu.CompilerParams(vmem_limit_bytes=4 << 20),
    )(*results)


def solution(mesh):
    torus = Mesh(mesh.devices.reshape(4, 4, 4, 4, 2), (*SEQ, *HEAD))
    placed = P(SEQ, HEAD)
    return jax.shard_map(
        per_device,
        mesh=torus,
        in_specs=(placed,) * 5,
        out_specs=(placed,) * 4,
        check_vma=False,
    )
```

```python
import functools
import itertools

import jax
import jax.numpy as jnp
from jax import lax
from jax.experimental import pallas as pl
from jax.experimental.pallas import tpu as pltpu
from jax.sharding import Mesh
from jax.sharding import PartitionSpec as P

DK = 128
BLOCK = 128
HEAD = ("head_0", "head_1")
SEQ = ("seq_0", "seq_1", "seq_2")
ID = pl.DeviceIdType.MESH
CHUNKS = 4
EARLY = 2
PIECES = 1

absmean_eps = 1e-05
norm_eps = 1e-06

f32 = jnp.float32
bf16 = jnp.bfloat16


def dot(a, b, contract):
    return lax.dot_general(a, b, ((contract[:1], contract[1:]), ((), ())), preferred_element_type=f32)


NN, NT, TN = (1, 0), (1, 1), (0, 0)


def exchange(axis, count, source, target, send, recv, shared=False):
    position = lax.axis_index(axis)
    copies = {}
    for kk in sorted(range(1, count), key=lambda kk: abs(2 * kk - count)):
        peer = lax.rem(position + kk, count)
        copy = pltpu.make_async_remote_copy(
            src_ref=source(peer),
            dst_ref=target(kk),
            send_sem=send if shared else send.at[kk - 1],
            recv_sem=recv if shared else recv.at[kk - 1],
            device_id={axis: peer},
            device_id_type=ID,
        )
        copy.start()
        copies[kk] = copy
    return [copies[kk] for kk in range(1, count)]


def arrive(copies):
    for copy in copies:
        copy.wait_recv()


def kernel(
    sizes, x_in, latent_in, q_in, k_in, go_in, attn_ref, gq_ref, gk_ref, gl_ref,
    latent_ref, q_ref, k_ref, go_ref, wa, wb, wt, xg, acc, v, sc, st, prior, within, gm, gs, following, gkp, gvp, gvt, loc, scan_send, scan_recv, zr, inc,
    pa, pb, ra1, rb1, sa2, sb2, ra2, rb2, tz, tzf, rz,
    own_sem, wz_s, wz_r, w2_s, w2_r, w3_s, w3_r, xp_s, xm_s, xs_s, xl_r, xs_r, scan_s, scan_r, zs_s, zs_r, g1_s, g1_r, g_s, g_r,
):
    ny, nx, nz, nl = sizes
    yy, xx, zh = (lax.axis_index(a) for a in SEQ)
    zl, cc = (lax.axis_index(a) for a in HEAD)
    tokens, feats = x_in.shape
    rows, columns = latent_ref.shape
    half = rows // 2
    heads = columns // DK
    blocks = tokens // BLOCK
    step = tokens // CHUNKS
    sent, left = [], []

    fetches = [
        pltpu.make_async_copy(latent_in, latent_ref, own_sem.at[0]),
        pltpu.make_async_copy(x_in, xg.at[zl, cc], own_sem.at[1]),
        pltpu.make_async_copy(q_in, q_ref, own_sem.at[2]),
        pltpu.make_async_copy(k_in, k_ref, own_sem.at[3]),
        pltpu.make_async_copy(go_in, go_ref, own_sem.at[4]),
    ]
    for fetch in fetches:
        fetch.start()
    at_a = (yy * nx + xx) * nz
    at_b = (xx * ny + yy) * nz
    barrier = pltpu.get_barrier_semaphore()
    for axis, count in (("seq_2", nz), ("seq_1", nx), ("seq_0", ny), ("head_1", 2)):
        position = lax.axis_index(axis)
        for kk in range(1, count):
            pl.semaphore_signal(
                barrier, inc=1, device_id={axis: lax.rem(position + kk, count)}, device_id_type=ID
            )

    @pl.when(zl > 0)
    def _():
        pl.semaphore_signal(barrier, inc=1, device_id={"head_0": zl - 1}, device_id_type=ID)

    @pl.when(zl < nl - 1)
    def _():
        pl.semaphore_signal(barrier, inc=1, device_id={"head_0": zl + 1}, device_id_type=ID)

    fetches[0].wait()
    latent16 = latent_ref[...].astype(bf16)
    wa[at_a + zh] = latent16[:half]
    wb[at_b + zh] = latent16[half:]
    fetches[1].wait()
    partners = (nz - 1) + (nx - 1) + (ny - 1) + 1
    neighbours = jnp.where(zl > 0, 1, 0) + jnp.where(zl < nl - 1, 1, 0)
    pl.semaphore_wait(barrier, partners + neighbours)

    up, down = lax.rem(zh + 1, nz), lax.rem(zh + nz - 1, nz)
    opposite = lax.rem(zh + 2, nz)

    def z_copy(peer, source, target, send, recv, alone=True):
        copy = pltpu.make_async_remote_copy(
            src_ref=source, dst_ref=target, send_sem=send, recv_sem=recv,
            device_id={"seq_2": peer}, device_id_type=ID,
        )
        copy.start()
        if alone:
            sent.append(copy)
        return copy

    def w_copy(peer, ref, at, n):
        return z_copy(peer, ref.at[at], ref.at[at], wz_s.at[n], wz_r.at[n])

    wz = [
        w_copy(up, wa, at_a + zh, 0),
        w_copy(down, wb, at_b + zh, 1),
        w_copy(up, wb, at_b + zh, 2),
        w_copy(down, wa, at_a + zh, 3),
    ]

    def rows_of(ref, j):
        return ref.at[pl.ds(pl.multiple_of(j * step, step), step)]

    def line_copy(block, j, up):
        place = rows_of(xg.at[block, cc], j)
        return pltpu.make_async_remote_copy(
            src_ref=place,
            dst_ref=place,
            send_sem=(xp_s if up else xm_s).at[block],
            recv_sem=xl_r.at[block, j],
            device_id={"head_0": zl + 1 if up else zl - 1},
            device_id_type=ID,
        )

    def side_copy(block, j):
        place = rows_of(xg.at[block, cc], j)
        return pltpu.make_async_remote_copy(
            src_ref=place,
            dst_ref=place,
            send_sem=xs_s.at[block],
            recv_sem=xs_r.at[block, j],
            device_id={"head_1": 1 - cc},
            device_id_type=ID,
        )

    def send_own(first, last):
        @pl.loop(first, last)
        def _(j):
            @pl.when(zl < nl - 1)
            def _():
                line_copy(zl, j, True).start()

            @pl.when(zl > 0)
            def _():
                line_copy(zl, j, False).start()

            side_copy(zl, j).start()

    send_own(0, EARLY)

    def relay(distance, first, last):
        @pl.loop(first, last)
        def _(j):
            @pl.when(zl >= distance)
            def _():
                block = zl - distance
                line_copy(block, j, True).wait_recv()

                @pl.when(zl < nl - 1)
                def _():
                    line_copy(block, j, True).start()

                side_copy(block, j).start()

            @pl.when(zl + distance < nl)
            def _():
                block = zl + distance
                line_copy(block, j, False).wait_recv()

                @pl.when(zl > 0)
                def _():
                    line_copy(block, j, False).start()

                side_copy(block, j).start()

    causal = lax.broadcasted_iota(jnp.int32, (BLOCK, BLOCK), 0) >= lax.broadcasted_iota(
        jnp.int32, (BLOCK, BLOCK), 1
    )

    def unrolled(body, first, last):
        for b in range(first, last):
            for i in range(heads):
                body(b, i, slice(b * BLOCK, (b + 1) * BLOCK), slice(i * DK, (i + 1) * DK))

    def each_block(body):
        @pl.loop(0, blocks)
        def _(b):
            at = pl.ds(pl.multiple_of(b * BLOCK, BLOCK), BLOCK)
            for i in range(heads):
                body(b, i, at, slice(i * DK, (i + 1) * DK))

    def scores_body(b, i, at, cols):
        s = dot(q_ref[at, cols], k_ref[at, cols], NT)
        sc[b, i] = jnp.where(causal, s, 0.0).astype(bf16)

    for fetch in fetches[2:]:
        fetch.wait()
    each_block(scores_body)

    wz[0].wait_recv()
    wz += [w_copy(up, wa, at_a + down, 4)]
    wz[1].wait_recv()
    wz += [w_copy(down, wb, at_b + up, 5)]
    send_own(EARLY, CHUNKS)
    relay(1, 0, CHUNKS // 2)
    arrive(wz[2:])
    mine_a = wa.at[pl.ds(at_a, nz)]
    mine_b = wb.at[pl.ds(at_b, nz)]
    w2a = exchange("seq_1", nx, lambda p: mine_a, lambda kk: mine_a, w2_s.at[0], w2_r.at[0])
    w2b = exchange("seq_0", ny, lambda p: mine_b, lambda kk: mine_b, w2_s.at[1], w2_r.at[1])
    sent += w2a + w2b
    relay(1, CHUNKS // 2, CHUNKS)
    row_a = wa.at[pl.ds(yy * nx * nz, nx * nz)]
    row_b = wb.at[pl.ds(xx * ny * nz, ny * nz)]
    arrive(w2a)
    w3a = exchange("seq_0", ny, lambda p: row_a, lambda kk: row_a, w3_s.at[0], w3_r.at[0])
    arrive(w2b)
    w3b = exchange("seq_1", nx, lambda p: row_b, lambda kk: row_b, w3_s.at[1], w3_r.at[1])
    sent += w3a + w3b
    for distance in range(2, nl - 1):
        relay(distance, 0, CHUNKS)
    arrive(w3a)
    arrive(w3b)
    far = nl - 1 - zl

    def at_end(body):
        pl.when(jnp.logical_or(zl == 0, zl == nl - 1))(body)

    def share_far(first, last):
        @at_end
        def _():
            @pl.loop(first, last)
            def _(j):
                line_copy(far, j, True).wait_recv()
                side_copy(far, j).start()

    share_far(0, 1)

    def magnitude(s, total):
        both = jnp.abs(wa[s].astype(f32)) + jnp.abs(wb[s].astype(f32))
        return total + both.reshape(half // 8, 8, columns).sum(axis=0)

    total = lax.fori_loop(0, ny * nx * nz, magnitude, jnp.zeros((8, columns), f32))
    scale = total.sum(axis=0, keepdims=True) / (ny * nx * nz * rows) + absmean_eps
    halfway = 0.5 * scale

    def ternary(w):
        w = w.astype(f32)
        return jnp.where(w > halfway, scale, jnp.where(w < -halfway, -scale, 0.0)).astype(bf16)

    @pl.loop(0, ny * nx)
    def _(p):
        other = lax.rem(p, nx) * ny + p // nx
        for z in range(nz):
            at = pl.multiple_of((p * nz + z) * rows, rows)
            wt[pl.ds(at, half)] = ternary(wa[p * nz + z])
            wt[pl.ds(pl.multiple_of(at + half, half), half)] = ternary(wb[other * nz + z])

    share_far(1, 2)
    acc[...] = jnp.zeros_like(acc)

    def features(block, core):
        return wt[pl.ds(pl.multiple_of((block * 2 + core) * feats, feats), feats)]

    @pl.loop(0, nl)
    def _(block):
        @pl.when(jnp.abs(block - zl) < nl - 1)
        def _():
            @pl.loop(0, CHUNKS)
            def _(j):
                side_copy(block, j).wait_recv()

            @pl.loop(0, 2)
            def _(core):
                acc[...] += dot(xg[block, core], features(block, core), NN)

    share_far(2, CHUNKS // 2 + 1)

    @at_end
    def _():
        half_at = pl.ds(0, tokens // 2)

        @pl.loop(0, CHUNKS // 2)
        def _(j):
            side_copy(far, j).wait_recv()

        acc[half_at] += dot(xg[far, cc, half_at], features(far, cc), NN)
        acc[half_at] += dot(xg[far, 1 - cc, half_at], features(far, 1 - cc), NN)

        def multiply(core, j):
            at = slice(j * step, (j + 1) * step)
            acc[at] += dot(xg[far, core, at], features(far, core), NN)

        for j in range(CHUNKS // 2, CHUNKS):
            if j > CHUNKS // 2:
                line_copy(far, j, True).wait_recv()
                side_copy(far, j).start()
                side_copy(far, j - 1).wait_recv()
                multiply(1 - cc, j - 1)
            multiply(cc, j)
        side_copy(far, CHUNKS - 1).wait_recv()
        multiply(1 - cc, CHUNKS - 1)

    def all_left(ref, semaphore):
        pltpu.make_async_remote_copy(
            src_ref=ref, dst_ref=ref, send_sem=semaphore, recv_sem=semaphore,
            device_id={"head_1": 1 - cc}, device_id_type=ID,
        ).wait_send()

    def all_arrived(ref, semaphore):
        pltpu.make_async_remote_copy(
            src_ref=ref, dst_ref=ref, send_sem=semaphore, recv_sem=semaphore,
            device_id={"head_1": 1 - cc}, device_id_type=ID,
        ).wait_recv()

    @pl.when(zl == nl - 2)
    def _():
        all_left(xg.at[0, cc], xp_s.at[0])

    @pl.when(zl == 1)
    def _():
        all_left(xg.at[nl - 1, cc], xm_s.at[nl - 1])

    v[...] = acc[...].astype(bf16)

    totals = [jnp.zeros((DK, DK), f32)] * heads

    def state_body(b, i, at, cols):
        s = dot(k_ref[at, cols], v[at, cols], TN)
        st[b, i] = s
        totals[i] = totals[i] + s

    unrolled(state_body, 0, blocks)
    for i in range(heads):
        loc[i] = totals[i]

    part = DK // PIECES
    tasks, serial = [], itertools.count()
    finished = {}

    def exchange_part(axis, count, which, i, r, stage, slot):
        copies = exchange(
            axis, count, lambda p: scan_send.at[which, i, r, slot], lambda kk: scan_recv.at[which, i, r, stage, kk - 1],
            scan_s.at[which, i, r, stage], scan_r.at[which, i, r, stage], True,
        )
        left.append((scan_send.at[which, i, r, 0 : count - 1], scan_s.at[which, i, r, stage]))
        return copies

    def collect(axis, count, which, i, r, stage, copies, mine):
        position = lax.axis_index(axis)
        before, everything = jnp.zeros((part, DK), f32), mine
        all_arrived(scan_recv.at[which, i, r, stage, 0 : count - 1], scan_r.at[which, i, r, stage])
        for kk in range(1, count):
            value = scan_recv[which, i, r, stage, kk - 1].astype(f32)
            sender = lax.rem(position + count - kk, count)
            before += jnp.where(earlier(which, sender, position), value, 0.0)
            everything += value
        return before, everything

    def earlier(which, p, mine):
        return p > mine if which else p < mine

    def step_z(which, i, r, n, peer, source, target):
        if n == 0:
            left.append((scan_send.at[which, i, r, 0 : nz - 1], zs_s.at[which, i, r]))
        return z_copy(peer, source, target, zs_s.at[which, i, r], zs_r.at[which, i, r], False)

    def chain_xyz(which, i, r, now):
        send, arrived = scan_send.at[which, i, r], zr.at[which, i, r]
        own = slice(r * part, (r + 1) * part)
        value = loc[i, own]
        send[0] = value.astype(bf16)
        copies = exchange_part("seq_1", nx, which, i, r, 0, 0)
        yield now + 3.3
        before, row = collect("seq_1", nx, which, i, r, 0, copies, value)
        send[1] = row.astype(bf16)
        copies = exchange_part("seq_0", ny, which, i, r, 1, 1)
        yield now + 6.4
        more, _ = collect("seq_0", ny, which, i, r, 1, copies, row)
        before += more
        send[2] = before.astype(bf16)
        send[3] = (before + loc[i, own]).astype(bf16)

        def message(peer):
            return send.at[2 + jnp.where(earlier(which, zh, peer), 1, 0)]

        for n, peer in ((0, opposite), (1, up), (2, down)):
            step_z(which, i, r, n, peer, message(peer), arrived.at[n])
        yield now + 14.4
        all_arrived(arrived, zs_r.at[which, i, r])
        inc[i, own] = before + arrived[0].astype(f32) + arrived[1].astype(f32) + arrived[2].astype(f32)
        done(which, now + 14.4)

    def chain_zxy(which, i, r, now):
        send, arrived = scan_send.at[which, i, r], zr.at[which, i, r]
        own = slice(r * part, (r + 1) * part)
        send[0] = loc[i, own].astype(bf16)
        for n, peer in ((0, opposite), (1, up), (2, down)):
            step_z(which, i, r, n, peer, send.at[0], arrived.at[n])
        yield now + 8.0
        before, line = jnp.zeros((part, DK), f32), loc[i, own]
        all_arrived(arrived, zs_r.at[which, i, r])
        for n, sender in ((0, opposite), (1, down), (2, up)):
            value = arrived[n].astype(f32)
            before += jnp.where(earlier(which, sender, zh), value, 0.0)
            line += value
        send[1] = line.astype(bf16)
        copies = exchange_part("seq_1", nx, which, i, r, 0, 1)
        yield now + 11.3
        more, plane = collect("seq_1", nx, which, i, r, 0, copies, line)
        before += more
        send[2] = plane.astype(bf16)
        copies = exchange_part("seq_0", ny, which, i, r, 1, 2)
        yield now + 14.6
        more, _ = collect("seq_0", ny, which, i, r, 1, copies, plane)
        inc[i, own] = before + more
        done(which, now + 14.6)

    def begin_scan(which, i, now):
        for r in range(PIECES):
            chain = chain_zxy if i % 2 else chain_xyz
            tasks.append((now + 0.01 * r, next(serial), chain(which, i, r, now + 0.5 * r)))

    def work(body, i, first, last):
        for b in range(first, last):
            body(b, i, slice(b * BLOCK, (b + 1) * BLOCK), slice(i * DK, (i + 1) * DK))
        return
        yield

    def later(now, body, i):
        for t in range(2):
            tasks.append((now + 0.7 * t, next(serial), work(body, i, blocks // 2 * t, blocks // 2 * (t + 1))))

    def done(which, now):
        finished[which] = finished.get(which, 0) + 1
        if finished[which] < PIECES * heads:
            return
        if which:
            for i in range(heads):
                follow(i)
            return
        forward()
        for i in reversed(range(heads)):
            begin_scan(1, i, now + 2.0)
        for i in range(heads):
            later(now + 2.1, backward_body, i)

    def within_body(b, i, at, cols):
        within[b, i] = dot(sc[b, i], v[at, cols], NN)

    def forward():
        places = [
            (b, i, slice(b * BLOCK, (b + 1) * BLOCK), slice(i * DK, (i + 1) * DK))
            for b in range(blocks)
            for i in range(heads)
        ]
        for i in range(heads):
            carried = inc[i]
            for b in range(blocks):
                prior[b, i] = carried.astype(bf16)
                carried = carried + st[b, i]
        for b, i, at, cols in places:
            within[b, i] += dot(q_ref[at, cols], prior[b, i], NN)
        for b, i, at, cols in places:
            mixed, upstream = within[b, i], go_ref[at, cols].astype(f32)
            inverse = 1.0 / jnp.sqrt(jnp.mean(mixed * mixed, axis=-1, keepdims=True) + norm_eps)
            inner = jnp.mean(upstream * mixed, axis=-1, keepdims=True) * inverse
            normed = mixed * inverse
            attn_ref[at, cols] = normed.astype(bf16)
            gm[at, cols] = ((upstream - normed * inner) * inverse).astype(bf16)
        for b, i, at, cols in places:
            gs[b, i] = dot(q_ref[at, cols], gm[at, cols], TN)
        for i in range(heads):
            total = gs[0, i]
            for b in range(1, blocks):
                total = total + gs[b, i]
            loc[i] = total

    def backward_body(b, i, at, cols):
        grad_mixed = gm[at, cols]
        grad_scores = jnp.where(causal, dot(grad_mixed, v[at, cols], NT), 0.0).astype(bf16)
        grad_query = dot(grad_scores, k_ref[at, cols], NN) + dot(grad_mixed, prior[b, i], NT)
        gq_ref[at, cols] = grad_query.astype(bf16)
        gkp[b, i] = dot(grad_scores, q_ref[at, cols], TN)
        gvp[b, i] = dot(sc[b, i], grad_mixed, TN)

    def follow(i):
        carried = inc[i]
        cols = slice(i * DK, (i + 1) * DK)
        for b in reversed(range(blocks)):
            at = slice(b * BLOCK, (b + 1) * BLOCK)
            following16 = carried.astype(bf16)
            following[b, i] = following16
            carried = carried + gs[b, i]
            grad_value = gvp[b, i] + dot(k_ref[at, cols], following16, NN)
            gvt[cols, at] = grad_value.T.astype(bf16)

    for i in range(heads):
        begin_scan(0, i, 0.0)
        later(0.1, within_body, i)
    while tasks:
        earliest = min(tasks)
        tasks.remove(earliest)
        expected = next(earliest[2], None)
        if expected is not None:
            tasks.append((expected, earliest[1], earliest[2]))

    piece = nz * rows
    side = columns // 2

    per_block = feats // piece
    order = []
    for k in (2, 1, 3, 0):
        order += [(dy, k) for dy in (2, 1, 3, 0)] + [(k, dx) for dx in (2, 1, 3, 0)]
    half_side = side // 2
    first, second_half = slice(0, half_side), slice(half_side, side)
    ring = {}

    def hop(which, k, n, forward, source, target):
        axis, position, count = (("seq_0", yy, ny), ("seq_1", xx, nx))[which]
        peer = lax.rem(position + (1 if forward else count - 1), count)
        copy = pltpu.make_async_remote_copy(
            src_ref=source, dst_ref=target,
            send_sem=g1_s.at[which, k], recv_sem=g1_r.at[which, k, min(n, 2)],
            device_id={axis: peer}, device_id_type=ID,
        )
        copy.start()
        ring[which, k, n] = copy

    def begin(which, distance, k, source, target):
        if distance == 2:
            hop(which, k, 0, True, source.at[first], target.at[2, k, first])
            hop(which, k, 1, False, source.at[second_half], target.at[2, k, second_half])
        elif distance == 1:
            hop(which, k, 2, True, source.at[second_half], target.at[0, k, second_half])
        elif distance == 3:
            hop(which, k, 3, False, source.at[first], target.at[1, k, first])

    def pass_on(which, k, ahead, behind, target):
        ring[which, k, 0].wait_recv()
        ahead[first] = (ahead[first].astype(f32) + target[2, k, first].astype(f32)).astype(bf16)
        hop(which, k, 4, True, ahead.at[first], target.at[0, k, first])
        ring[which, k, 1].wait_recv()
        behind[second_half] = (behind[second_half].astype(f32) + target[2, k, second_half].astype(f32)).astype(bf16)
        hop(which, k, 5, False, behind.at[second_half], target.at[1, k, second_half])

    def pass_both(k):
        pass_on(0, k, pa.at[1, k], pa.at[3, k], ra1)
        pass_on(1, k, pb.at[k, 1], pb.at[k, 3], rb1)

    for n, (dy, dx) in enumerate(dict.fromkeys(order)):
        to_y, to_x = lax.rem(yy + dy, ny), lax.rem(xx + dx, nx)
        p = to_y * nx + to_x
        block = p // per_block
        lanes = pl.ds(pl.multiple_of(lax.rem(p, per_block) * piece, piece), piece)
        term = dot(gvt[...], xg[block // 2, lax.rem(block, 2), :, lanes], NN).astype(bf16)
        pa[dy, dx] = term[:side]
        pb[dy, dx] = term[side:]
        begin(0, dy, dx, pa.at[dy, dx], ra1)
        begin(1, dx, dy, pb.at[dy, dx], rb1)
        if n == 11:
            pass_both(2)
    left += [(ref.at[0:3, 0], g1_s.at[which, k]) for which, ref in ((0, pa), (1, pb)) for k in range(4)]

    def summed_a(dx):
        value = pa[0, dx].astype(f32)
        all_arrived(ra1.at[0:2, dx], g1_r.at[0, dx, 2])
        return value + ra1[0, dx].astype(f32) + ra1[1, dx].astype(f32)

    def summed_b(dy):
        value = pb[dy, 0].astype(f32)
        all_arrived(rb1.at[0:2, dy], g1_r.at[1, dy, 2])
        return value + rb1[0, dy].astype(f32) + rb1[1, dy].astype(f32)

    def second(axis, position, count, k, source, target, which):
        copy = pltpu.make_async_remote_copy(
            src_ref=source.at[k - 1], dst_ref=target.at[k - 1],
            send_sem=g_s.at[which], recv_sem=g_r.at[which],
            device_id={axis: lax.rem(position + k, count)}, device_id_type=ID,
        )
        copy.start()

    left += [(sa2, g_s.at[0]), (sb2, g_s.at[1])]

    def second_both(k):
        sa2[k - 1] = summed_a(k).astype(bf16)
        second("seq_1", xx, nx, k, sa2, ra2, 0)
        sb2[k - 1] = summed_b(k).astype(bf16)
        second("seq_0", yy, ny, k, sb2, rb2, 1)

    pass_both(1)
    second_both(2)
    pass_both(3)
    second_both(1)
    pass_both(0)
    second_both(3)

    def key_body(b, i, at, cols):
        grad_key = gkp[b, i] + dot(v[at, cols], following[b, i], NT)
        gk_ref[at, cols] = grad_key.astype(bf16)

    each_block(key_body)

    final_a, final_b = summed_a(0), summed_b(0)

    def last(final, received, which):
        all_arrived(received, g_r.at[which])
        for kk in range(received.shape[0]):
            final += received[kk].astype(f32)
        final = final.T
        tzf[which] = final
        tz[which] = final.astype(bf16)
        left.append((tz.at[which, 0 : (nz - 1) * rows], g_s.at[2 + which]))
        exchange(
            "seq_2", nz, lambda p: tz.at[which, pl.ds(pl.multiple_of(p * rows, rows), rows)],
            lambda kk: rz.at[which, kk - 1], g_s.at[2 + which], g_r.at[2 + which], True,
        )

    last(final_a, ra2, 0)
    last(final_b, rb2, 1)
    for which in range(2):
        result = tzf[which, pl.ds(pl.multiple_of(zh * rows, rows), rows)]
        all_arrived(rz.at[which], g_r.at[2 + which])
        for kk in range(nz - 1):
            result += rz[which, kk].astype(f32)
        gl_ref[:, which * side : (which + 1) * side] = result

    for copy in sent:
        copy.wait_send()

    for ref, semaphore in left:
        all_left(ref, semaphore)

    @pl.loop(0, nl)
    def _(block):
        place = xg.at[block, cc]
        all_left(place, xs_s.at[block])
        ahead = jnp.logical_and(zl == nl - 2, block == 0)
        behind = jnp.logical_and(zl == 1, block == nl - 1)

        @pl.when(jnp.logical_and(jnp.logical_and(block <= zl, zl < nl - 1), jnp.logical_not(ahead)))
        def _():
            all_left(place, xp_s.at[block])

        @pl.when(jnp.logical_and(jnp.logical_and(block >= zl, zl > 0), jnp.logical_not(behind)))
        def _():
            all_left(place, xm_s.at[block])


def deliver(*refs):
    copies = [pltpu.make_async_copy(refs[i], refs[4 + i], refs[8].at[i]) for i in range(4)]
    for copy in copies:
        copy.start()
    for copy in copies:
        copy.wait()


def per_device(inputs, latent, queries, keys, grad_out):
    sizes = tuple(lax.axis_size(a) for a in (*SEQ, "head_0"))
    ny, nx, nz, nl = sizes
    tokens, feats = inputs.shape
    rows, columns = latent.shape
    heads, blocks = columns // DK, tokens // BLOCK
    seqs, everyone = ny * nx * nz, ny * nx * nz * rows
    side, piece = columns // 2, nz * rows
    dma = pltpu.SemaphoreType.DMA
    most = max(ny, nx, nz) - 1
    scratch = [
        pltpu.VMEM(latent.shape, f32),
        pltpu.VMEM((tokens, columns), bf16),
        pltpu.VMEM((tokens, columns), bf16),
        pltpu.VMEM((tokens, columns), bf16),
        pltpu.VMEM((seqs, rows // 2, columns), bf16),
        pltpu.VMEM((seqs, rows // 2, columns), bf16),
        pltpu.VMEM((everyone, columns), bf16),
        pltpu.VMEM((nl, 2, tokens, feats), bf16),
        pltpu.VMEM((tokens, columns), f32),
        pltpu.VMEM((tokens, columns), bf16),
        pltpu.VMEM((blocks, heads, BLOCK, BLOCK), bf16),
        pltpu.VMEM((blocks, heads, DK, DK), f32),
        pltpu.VMEM((blocks, heads, DK, DK), bf16),
        pltpu.VMEM((blocks, heads, BLOCK, DK), f32),
        pltpu.VMEM((tokens, columns), bf16),
        pltpu.VMEM((blocks, heads, DK, DK), f32),
        pltpu.VMEM((blocks, heads, DK, DK), bf16),
        pltpu.VMEM((blocks, heads, BLOCK, DK), f32),
        pltpu.VMEM((blocks, heads, BLOCK, DK), f32),
        pltpu.VMEM((columns, tokens), bf16),
        pltpu.VMEM((heads, DK, DK), f32),
        pltpu.VMEM((2, heads, PIECES, 4, DK // PIECES, DK), bf16),
        pltpu.VMEM((2, heads, PIECES, 2, most, DK // PIECES, DK), bf16),
        pltpu.VMEM((2, heads, PIECES, 3, DK // PIECES, DK), bf16),
        pltpu.VMEM((heads, DK, DK), f32),
        pltpu.VMEM((ny, nx, side, piece), bf16),
        pltpu.VMEM((ny, nx, side, piece), bf16),
        pltpu.VMEM((ny - 1, nx, side, piece), bf16),
        pltpu.VMEM((nx - 1, ny, side, piece), bf16),
        pltpu.VMEM((nx - 1, side, piece), bf16),
        pltpu.VMEM((ny - 1, side, piece), bf16),
        pltpu.VMEM((nx - 1, side, piece), bf16),
        pltpu.VMEM((ny - 1, side, piece), bf16),
        pltpu.VMEM((2, piece, side), bf16),
        pltpu.VMEM((2, piece, side), f32),
        pltpu.VMEM((2, nz - 1, rows, side), bf16),
        dma((5,)),
        dma((6,)), dma((6,)),
        dma((2, most)), dma((2, most)),
        dma((2, most)), dma((2, most)),
        dma((nl,)), dma((nl,)), dma((nl,)),
        dma((nl, CHUNKS)), dma((nl, CHUNKS)),
        dma((2, heads, PIECES, 2)), dma((2, heads, PIECES, 2)),
        dma((2, heads, PIECES)), dma((2, heads, PIECES)),
        dma((2, 4)), dma((2, 4, 3)),
        dma((4,)), dma((4,)),
    ]
    like = jax.ShapeDtypeStruct(queries.shape, bf16)
    results = pl.pallas_call(
        functools.partial(kernel, sizes),
        out_shape=(like, like, like, jax.ShapeDtypeStruct(latent.shape, f32)),
        in_specs=[pl.BlockSpec(memory_space=pltpu.HBM)] * 5,
        out_specs=(pl.BlockSpec(memory_space=pltpu.VMEM),) * 4,
        scratch_shapes=scratch,
        compiler_params=pltpu.CompilerParams(
            collective_id=0, has_side_effects=True, vmem_limit_bytes=40 << 20
        ),
    )(*(pltpu.with_memory_space_constraint(a, pltpu.HBM) for a in (inputs, latent, queries, keys, grad_out)))
    return pl.pallas_call(
        deliver,
        out_shape=(like, like, like, jax.ShapeDtypeStruct(latent.shape, f32)),
        in_specs=[pl.BlockSpec(memory_space=pltpu.VMEM)] * 4,
        out_specs=(pl.BlockSpec(memory_space=pltpu.HBM),) * 4,
        scratch_shapes=[pltpu.SemaphoreType.DMA((4,))],
        compiler_params=pltpu.CompilerParams(vmem_limit_bytes=4 << 20),
    )(*results)


def solution(mesh):
    torus = Mesh(mesh.devices.reshape(4, 4, 4, 4, 2), (*SEQ, *HEAD))
    placed = P(SEQ, HEAD)
    return jax.shard_map(
        per_device,
        mesh=torus,
        in_specs=(placed,) * 5,
        out_specs=(placed,) * 4,
        check_vma=False,
    )
```

```python
import functools
import itertools

import jax
import jax.numpy as jnp
from jax import lax
from jax.experimental import pallas as pl
from jax.experimental.pallas import tpu as pltpu
from jax.sharding import Mesh
from jax.sharding import PartitionSpec as P

DK = 128
BLOCK = 128
HEAD = ("head_0", "head_1")
SEQ = ("seq_0", "seq_1", "seq_2")
ID = pl.DeviceIdType.MESH
CHUNKS = 4
EARLY = 2
PIECES = 1

absmean_eps = 1e-05
norm_eps = 1e-06

f32 = jnp.float32
bf16 = jnp.bfloat16


def dot(a, b, contract):
    return lax.dot_general(a, b, ((contract[:1], contract[1:]), ((), ())), preferred_element_type=f32)


NN, NT, TN = (1, 0), (1, 1), (0, 0)


def exchange(axis, count, source, target, send, recv, shared=False):
    position = lax.axis_index(axis)
    copies = {}
    for kk in sorted(range(1, count), key=lambda kk: abs(2 * kk - count)):
        peer = lax.rem(position + kk, count)
        copy = pltpu.make_async_remote_copy(
            src_ref=source(peer),
            dst_ref=target(kk),
            send_sem=send if shared else send.at[kk - 1],
            recv_sem=recv if shared else recv.at[kk - 1],
            device_id={axis: peer},
            device_id_type=ID,
        )
        copy.start()
        copies[kk] = copy
    return [copies[kk] for kk in range(1, count)]


def arrive(copies):
    for copy in copies:
        copy.wait_recv()


def kernel(
    sizes, x_in, latent_in, q_in, k_in, go_in, attn_ref, gq_ref, gk_ref, gl_ref,
    latent_ref, q_ref, k_ref, go_ref, wa, wb, wt, xg, acc, v, sc, st, prior, within, gm, gs, following, gkp, gvp, gvt, loc, scan_send, scan_recv, zr, inc,
    pa, pb, ra1, rb1, sa2, sb2, ra2, rb2, tz, tzf, rz,
    own_sem, wz_s, wz_r, w2_s, w2_r, w3_s, w3_r, xp_s, xm_s, xs_s, xl_r, xs_r, scan_s, scan_r, zs_s, zs_r, g1_s, g1_r, g_s, g_r,
):
    ny, nx, nz, nl = sizes
    yy, xx, zh = (lax.axis_index(a) for a in SEQ)
    zl, cc = (lax.axis_index(a) for a in HEAD)
    tokens, feats = x_in.shape
    rows, columns = latent_ref.shape
    half = rows // 2
    heads = columns // DK
    blocks = tokens // BLOCK
    step = tokens // CHUNKS
    sent, left = [], []

    fetches = [
        pltpu.make_async_copy(latent_in, latent_ref, own_sem.at[0]),
        pltpu.make_async_copy(x_in, xg.at[zl, cc], own_sem.at[1]),
        pltpu.make_async_copy(q_in, q_ref, own_sem.at[2]),
        pltpu.make_async_copy(k_in, k_ref, own_sem.at[3]),
        pltpu.make_async_copy(go_in, go_ref, own_sem.at[4]),
    ]
    for fetch in fetches:
        fetch.start()
    at_a = (yy * nx + xx) * nz
    at_b = (xx * ny + yy) * nz
    barrier = pltpu.get_barrier_semaphore()
    for axis, count in (("seq_2", nz), ("seq_1", nx), ("seq_0", ny), ("head_1", 2)):
        position = lax.axis_index(axis)
        for kk in range(1, count):
            pl.semaphore_signal(
                barrier, inc=1, device_id={axis: lax.rem(position + kk, count)}, device_id_type=ID
            )

    @pl.when(zl > 0)
    def _():
        pl.semaphore_signal(barrier, inc=1, device_id={"head_0": zl - 1}, device_id_type=ID)

    @pl.when(zl < nl - 1)
    def _():
        pl.semaphore_signal(barrier, inc=1, device_id={"head_0": zl + 1}, device_id_type=ID)

    fetches[0].wait()
    latent16 = latent_ref[...].astype(bf16)
    wa[at_a + zh] = latent16[:half]
    wb[at_b + zh] = latent16[half:]
    fetches[1].wait()
    partners = (nz - 1) + (nx - 1) + (ny - 1) + 1
    neighbours = jnp.where(zl > 0, 1, 0) + jnp.where(zl < nl - 1, 1, 0)
    pl.semaphore_wait(barrier, partners + neighbours)

    up, down = lax.rem(zh + 1, nz), lax.rem(zh + nz - 1, nz)
    opposite = lax.rem(zh + 2, nz)

    def z_copy(peer, source, target, send, recv, alone=True):
        copy = pltpu.make_async_remote_copy(
            src_ref=source, dst_ref=target, send_sem=send, recv_sem=recv,
            device_id={"seq_2": peer}, device_id_type=ID,
        )
        copy.start()
        if alone:
            sent.append(copy)
        return copy

    def w_copy(peer, ref, at, n):
        return z_copy(peer, ref.at[at], ref.at[at], wz_s.at[n], wz_r.at[n])

    wz = [
        w_copy(up, wa, at_a + zh, 0),
        w_copy(down, wb, at_b + zh, 1),
        w_copy(up, wb, at_b + zh, 2),
        w_copy(down, wa, at_a + zh, 3),
    ]

    def all_left(ref, semaphore):
        pltpu.make_async_remote_copy(
            src_ref=ref, dst_ref=ref, send_sem=semaphore, recv_sem=semaphore,
            device_id={"head_1": 1 - cc}, device_id_type=ID,
        ).wait_send()

    def all_arrived(ref, semaphore):
        pltpu.make_async_remote_copy(
            src_ref=ref, dst_ref=ref, send_sem=semaphore, recv_sem=semaphore,
            device_id={"head_1": 1 - cc}, device_id_type=ID,
        ).wait_recv()

    def rows_of(ref, j):
        return ref.at[pl.ds(pl.multiple_of(j * step, step), step)]

    def line_copy(block, j, up):
        place = rows_of(xg.at[block, cc], j)
        return pltpu.make_async_remote_copy(
            src_ref=place,
            dst_ref=place,
            send_sem=(xp_s if up else xm_s).at[block],
            recv_sem=xl_r.at[block, j],
            device_id={"head_0": zl + 1 if up else zl - 1},
            device_id_type=ID,
        )

    def side_copy(block, j):
        place = rows_of(xg.at[block, cc], j)
        return pltpu.make_async_remote_copy(
            src_ref=place,
            dst_ref=place,
            send_sem=xs_s.at[block],
            recv_sem=xs_r.at[block, j],
            device_id={"head_1": 1 - cc},
            device_id_type=ID,
        )

    def send_own(first, last):
        @pl.loop(first, last)
        def _(j):
            @pl.when(zl < nl - 1)
            def _():
                line_copy(zl, j, True).start()

            @pl.when(zl > 0)
            def _():
                line_copy(zl, j, False).start()

            side_copy(zl, j).start()

    send_own(0, EARLY)

    def relay(distance, first, last):
        @pl.loop(first, last)
        def _(j):
            @pl.when(zl >= distance)
            def _():
                block = zl - distance
                line_copy(block, j, True).wait_recv()

                @pl.when(zl < nl - 1)
                def _():
                    line_copy(block, j, True).start()

                side_copy(block, j).start()

            @pl.when(zl + distance < nl)
            def _():
                block = zl + distance
                line_copy(block, j, False).wait_recv()

                @pl.when(zl > 0)
                def _():
                    line_copy(block, j, False).start()

                side_copy(block, j).start()

    causal = lax.broadcasted_iota(jnp.int32, (BLOCK, BLOCK), 0) >= lax.broadcasted_iota(
        jnp.int32, (BLOCK, BLOCK), 1
    )

    def unrolled(body, first, last):
        for b in range(first, last):
            for i in range(heads):
                body(b, i, slice(b * BLOCK, (b + 1) * BLOCK), slice(i * DK, (i + 1) * DK))

    def each_block(body):
        @pl.loop(0, blocks)
        def _(b):
            at = pl.ds(pl.multiple_of(b * BLOCK, BLOCK), BLOCK)
            for i in range(heads):
                body(b, i, at, slice(i * DK, (i + 1) * DK))

    def scores_body(b, i, at, cols):
        s = dot(q_ref[at, cols], k_ref[at, cols], NT)
        sc[b, i] = jnp.where(causal, s, 0.0).astype(bf16)

    for fetch in fetches[2:]:
        fetch.wait()
    each_block(scores_body)

    wz[0].wait_recv()
    wz += [w_copy(up, wa, at_a + down, 4)]
    wz[1].wait_recv()
    wz += [w_copy(down, wb, at_b + up, 5)]
    send_own(EARLY, CHUNKS)
    relay(1, 0, CHUNKS // 2)
    arrive(wz[2:])
    mine_a = wa.at[pl.ds(at_a, nz)]
    mine_b = wb.at[pl.ds(at_b, nz)]
    exchange("seq_1", nx, lambda p: mine_a, lambda kk: mine_a, w2_s.at[0], w2_r.at[0], True)
    exchange("seq_0", ny, lambda p: mine_b, lambda kk: mine_b, w2_s.at[1], w2_r.at[1], True)
    left += [(wa.at[0 : 3 * nz], w2_s.at[0]), (wb.at[0 : 3 * nz], w2_s.at[1])]
    relay(1, CHUNKS // 2, CHUNKS)
    row_a = wa.at[pl.ds(yy * nx * nz, nx * nz)]
    row_b = wb.at[pl.ds(xx * ny * nz, ny * nz)]
    all_arrived(wa.at[0 : 3 * nz], w2_r.at[0])
    exchange("seq_0", ny, lambda p: row_a, lambda kk: row_a, w3_s.at[0], w3_r.at[0], True)
    all_arrived(wb.at[0 : 3 * nz], w2_r.at[1])
    exchange("seq_1", nx, lambda p: row_b, lambda kk: row_b, w3_s.at[1], w3_r.at[1], True)
    left += [(wa.at[0 : 3 * nx * nz], w3_s.at[0]), (wb.at[0 : 3 * ny * nz], w3_s.at[1])]
    for distance in range(2, nl - 1):
        relay(distance, 0, CHUNKS)
    all_arrived(wa.at[0 : 3 * nx * nz], w3_r.at[0])
    all_arrived(wb.at[0 : 3 * ny * nz], w3_r.at[1])
    far = nl - 1 - zl

    def at_end(body):
        pl.when(jnp.logical_or(zl == 0, zl == nl - 1))(body)

    def share_far(first, last):
        @at_end
        def _():
            @pl.loop(first, last)
            def _(j):
                line_copy(far, j, True).wait_recv()
                side_copy(far, j).start()

    share_far(0, 1)

    def magnitude(s, total):
        both = jnp.abs(wa[s].astype(f32)) + jnp.abs(wb[s].astype(f32))
        return total + both.reshape(half // 8, 8, columns).sum(axis=0)

    total = lax.fori_loop(0, ny * nx * nz, magnitude, jnp.zeros((8, columns), f32))
    scale = total.sum(axis=0, keepdims=True) / (ny * nx * nz * rows) + absmean_eps
    halfway = 0.5 * scale

    def ternary(w):
        w = w.astype(f32)
        return jnp.where(w > halfway, scale, jnp.where(w < -halfway, -scale, 0.0)).astype(bf16)

    @pl.loop(0, ny * nx)
    def _(p):
        other = lax.rem(p, nx) * ny + p // nx
        for z in range(nz):
            at = pl.multiple_of((p * nz + z) * rows, rows)
            wt[pl.ds(at, half)] = ternary(wa[p * nz + z])
            wt[pl.ds(pl.multiple_of(at + half, half), half)] = ternary(wb[other * nz + z])

    share_far(1, 2)
    acc[...] = jnp.zeros_like(acc)

    def features(block, core):
        return wt[pl.ds(pl.multiple_of((block * 2 + core) * feats, feats), feats)]

    @pl.loop(0, nl)
    def _(block):
        @pl.when(jnp.abs(block - zl) < nl - 1)
        def _():
            @pl.loop(0, CHUNKS)
            def _(j):
                side_copy(block, j).wait_recv()

            @pl.loop(0, 2)
            def _(core):
                acc[...] += dot(xg[block, core], features(block, core), NN)

    share_far(2, CHUNKS // 2 + 1)

    @at_end
    def _():
        half_at = pl.ds(0, tokens // 2)

        @pl.loop(0, CHUNKS // 2)
        def _(j):
            side_copy(far, j).wait_recv()

        acc[half_at] += dot(xg[far, cc, half_at], features(far, cc), NN)
        acc[half_at] += dot(xg[far, 1 - cc, half_at], features(far, 1 - cc), NN)

        def multiply(core, j):
            at = slice(j * step, (j + 1) * step)
            acc[at] += dot(xg[far, core, at], features(far, core), NN)

        for j in range(CHUNKS // 2, CHUNKS):
            if j > CHUNKS // 2:
                line_copy(far, j, True).wait_recv()
                side_copy(far, j).start()
                side_copy(far, j - 1).wait_recv()
                multiply(1 - cc, j - 1)
            multiply(cc, j)
        side_copy(far, CHUNKS - 1).wait_recv()
        multiply(1 - cc, CHUNKS - 1)

    @pl.when(zl == nl - 2)
    def _():
        all_left(xg.at[0, cc], xp_s.at[0])

    @pl.when(zl == 1)
    def _():
        all_left(xg.at[nl - 1, cc], xm_s.at[nl - 1])

    v[...] = acc[...].astype(bf16)

    totals = [jnp.zeros((DK, DK), f32)] * heads

    def state_body(b, i, at, cols):
        s = dot(k_ref[at, cols], v[at, cols], TN)
        st[b, i] = s
        totals[i] = totals[i] + s

    unrolled(state_body, 0, blocks)
    for i in range(heads):
        loc[i] = totals[i]

    part = DK // PIECES
    tasks, serial = [], itertools.count()
    finished = {}

    def exchange_part(axis, count, which, i, r, stage, slot):
        copies = exchange(
            axis, count, lambda p: scan_send.at[which, i, r, slot], lambda kk: scan_recv.at[which, i, r, stage, kk - 1],
            scan_s.at[which, i, r, stage], scan_r.at[which, i, r, stage], True,
        )
        left.append((scan_send.at[which, i, r, 0 : count - 1], scan_s.at[which, i, r, stage]))
        return copies

    def collect(axis, count, which, i, r, stage, copies, mine):
        position = lax.axis_index(axis)
        before, everything = jnp.zeros((part, DK), f32), mine
        all_arrived(scan_recv.at[which, i, r, stage, 0 : count - 1], scan_r.at[which, i, r, stage])
        for kk in range(1, count):
            value = scan_recv[which, i, r, stage, kk - 1].astype(f32)
            sender = lax.rem(position + count - kk, count)
            before += jnp.where(earlier(which, sender, position), value, 0.0)
            everything += value
        return before, everything

    def earlier(which, p, mine):
        return p > mine if which else p < mine

    def step_z(which, i, r, n, peer, source, target):
        if n == 0:
            left.append((scan_send.at[which, i, r, 0 : nz - 1], zs_s.at[which, i, r]))
        return z_copy(peer, source, target, zs_s.at[which, i, r], zs_r.at[which, i, r], False)

    def chain_xyz(which, i, r, now):
        send, arrived = scan_send.at[which, i, r], zr.at[which, i, r]
        own = slice(r * part, (r + 1) * part)
        value = loc[i, own]
        send[0] = value.astype(bf16)
        copies = exchange_part("seq_1", nx, which, i, r, 0, 0)
        yield now + 3.3
        before, row = collect("seq_1", nx, which, i, r, 0, copies, value)
        send[1] = row.astype(bf16)
        copies = exchange_part("seq_0", ny, which, i, r, 1, 1)
        yield now + 6.4
        more, _ = collect("seq_0", ny, which, i, r, 1, copies, row)
        before += more
        send[2] = before.astype(bf16)
        send[3] = (before + loc[i, own]).astype(bf16)

        def message(peer):
            return send.at[2 + jnp.where(earlier(which, zh, peer), 1, 0)]

        for n, peer in ((0, opposite), (1, up), (2, down)):
            step_z(which, i, r, n, peer, message(peer), arrived.at[n])
        yield now + 14.4
        all_arrived(arrived, zs_r.at[which, i, r])
        inc[i, own] = before + arrived[0].astype(f32) + arrived[1].astype(f32) + arrived[2].astype(f32)
        done(which, now + 14.4)

    def chain_zxy(which, i, r, now):
        send, arrived = scan_send.at[which, i, r], zr.at[which, i, r]
        own = slice(r * part, (r + 1) * part)
        send[0] = loc[i, own].astype(bf16)
        for n, peer in ((0, opposite), (1, up), (2, down)):
            step_z(which, i, r, n, peer, send.at[0], arrived.at[n])
        yield now + 8.0
        before, line = jnp.zeros((part, DK), f32), loc[i, own]
        all_arrived(arrived, zs_r.at[which, i, r])
        for n, sender in ((0, opposite), (1, down), (2, up)):
            value = arrived[n].astype(f32)
            before += jnp.where(earlier(which, sender, zh), value, 0.0)
            line += value
        send[1] = line.astype(bf16)
        copies = exchange_part("seq_1", nx, which, i, r, 0, 1)
        yield now + 11.3
        more, plane = collect("seq_1", nx, which, i, r, 0, copies, line)
        before += more
        send[2] = plane.astype(bf16)
        copies = exchange_part("seq_0", ny, which, i, r, 1, 2)
        yield now + 14.6
        more, _ = collect("seq_0", ny, which, i, r, 1, copies, plane)
        inc[i, own] = before + more
        done(which, now + 14.6)

    def begin_scan(which, i, now):
        for r in range(PIECES):
            chain = chain_zxy if i % 2 else chain_xyz
            tasks.append((now + 0.01 * r, next(serial), chain(which, i, r, now + 0.5 * r)))

    def work(body, i, first, last):
        for b in range(first, last):
            body(b, i, slice(b * BLOCK, (b + 1) * BLOCK), slice(i * DK, (i + 1) * DK))
        return
        yield

    def later(now, body, i):
        for t in range(2):
            tasks.append((now + 0.7 * t, next(serial), work(body, i, blocks // 2 * t, blocks // 2 * (t + 1))))

    def done(which, now):
        finished[which] = finished.get(which, 0) + 1
        if finished[which] < PIECES * heads:
            return
        if which:
            for i in range(heads):
                follow(i)
            return
        forward()
        for i in reversed(range(heads)):
            begin_scan(1, i, now + 2.0)
        for i in range(heads):
            later(now + 2.1, backward_body, i)

    def within_body(b, i, at, cols):
        within[b, i] = dot(sc[b, i], v[at, cols], NN)

    def forward():
        places = [
            (b, i, slice(b * BLOCK, (b + 1) * BLOCK), slice(i * DK, (i + 1) * DK))
            for b in range(blocks)
            for i in range(heads)
        ]
        for i in range(heads):
            carried = inc[i]
            for b in range(blocks):
                prior[b, i] = carried.astype(bf16)
                carried = carried + st[b, i]
        for b, i, at, cols in places:
            within[b, i] += dot(q_ref[at, cols], prior[b, i], NN)
        for b, i, at, cols in places:
            mixed, upstream = within[b, i], go_ref[at, cols].astype(f32)
            inverse = 1.0 / jnp.sqrt(jnp.mean(mixed * mixed, axis=-1, keepdims=True) + norm_eps)
            inner = jnp.mean(upstream * mixed, axis=-1, keepdims=True) * inverse
            normed = mixed * inverse
            attn_ref[at, cols] = normed.astype(bf16)
            gm[at, cols] = ((upstream - normed * inner) * inverse).astype(bf16)
        for b, i, at, cols in places:
            gs[b, i] = dot(q_ref[at, cols], gm[at, cols], TN)
        for i in range(heads):
            total = gs[0, i]
            for b in range(1, blocks):
                total = total + gs[b, i]
            loc[i] = total

    def backward_body(b, i, at, cols):
        grad_mixed = gm[at, cols]
        grad_scores = jnp.where(causal, dot(grad_mixed, v[at, cols], NT), 0.0).astype(bf16)
        grad_query = dot(grad_scores, k_ref[at, cols], NN) + dot(grad_mixed, prior[b, i], NT)
        gq_ref[at, cols] = grad_query.astype(bf16)
        gkp[b, i] = dot(grad_scores, q_ref[at, cols], TN)
        gvp[b, i] = dot(sc[b, i], grad_mixed, TN)

    def follow(i):
        carried = inc[i]
        cols = slice(i * DK, (i + 1) * DK)
        for b in reversed(range(blocks)):
            at = slice(b * BLOCK, (b + 1) * BLOCK)
            following16 = carried.astype(bf16)
            following[b, i] = following16
            carried = carried + gs[b, i]
            grad_value = gvp[b, i] + dot(k_ref[at, cols], following16, NN)
            gvt[cols, at] = grad_value.T.astype(bf16)

    for i in range(heads):
        begin_scan(0, i, 0.0)
        later(0.1, within_body, i)
    while tasks:
        earliest = min(tasks)
        tasks.remove(earliest)
        expected = next(earliest[2], None)
        if expected is not None:
            tasks.append((expected, earliest[1], earliest[2]))

    piece = nz * rows
    side = columns // 2

    per_block = feats // piece
    order = []
    for k in (2, 1, 3, 0):
        order += [(dy, k) for dy in (2, 1, 3, 0)] + [(k, dx) for dx in (2, 1, 3, 0)]
    half_side = side // 2
    first, second_half = slice(0, half_side), slice(half_side, side)
    ring = {}

    def hop(which, k, n, forward, source, target):
        axis, position, count = (("seq_0", yy, ny), ("seq_1", xx, nx))[which]
        peer = lax.rem(position + (1 if forward else count - 1), count)
        copy = pltpu.make_async_remote_copy(
            src_ref=source, dst_ref=target,
            send_sem=g1_s.at[which, k], recv_sem=g1_r.at[which, k, min(n, 2)],
            device_id={axis: peer}, device_id_type=ID,
        )
        copy.start()
        ring[which, k, n] = copy

    def begin(which, distance, k, source, target):
        if distance == 2:
            hop(which, k, 0, True, source.at[first], target.at[2, k, first])
            hop(which, k, 1, False, source.at[second_half], target.at[2, k, second_half])
        elif distance == 1:
            hop(which, k, 2, True, source.at[second_half], target.at[0, k, second_half])
        elif distance == 3:
            hop(which, k, 3, False, source.at[first], target.at[1, k, first])

    def pass_on(which, k, ahead, behind, target):
        ring[which, k, 0].wait_recv()
        ahead[first] = (ahead[first].astype(f32) + target[2, k, first].astype(f32)).astype(bf16)
        hop(which, k, 4, True, ahead.at[first], target.at[0, k, first])
        ring[which, k, 1].wait_recv()
        behind[second_half] = (behind[second_half].astype(f32) + target[2, k, second_half].astype(f32)).astype(bf16)
        hop(which, k, 5, False, behind.at[second_half], target.at[1, k, second_half])

    def pass_both(k):
        pass_on(0, k, pa.at[1, k], pa.at[3, k], ra1)
        pass_on(1, k, pb.at[k, 1], pb.at[k, 3], rb1)

    for n, (dy, dx) in enumerate(dict.fromkeys(order)):
        to_y, to_x = lax.rem(yy + dy, ny), lax.rem(xx + dx, nx)
        p = to_y * nx + to_x
        block = p // per_block
        lanes = pl.ds(pl.multiple_of(lax.rem(p, per_block) * piece, piece), piece)
        term = dot(gvt[...], xg[block // 2, lax.rem(block, 2), :, lanes], NN).astype(bf16)
        pa[dy, dx] = term[:side]
        pb[dy, dx] = term[side:]
        begin(0, dy, dx, pa.at[dy, dx], ra1)
        begin(1, dx, dy, pb.at[dy, dx], rb1)
        if n == 11:
            pass_both(2)
    left += [(ref.at[0:3, 0], g1_s.at[which, k]) for which, ref in ((0, pa), (1, pb)) for k in range(4)]

    def summed_a(dx):
        value = pa[0, dx].astype(f32)
        all_arrived(ra1.at[0:2, dx], g1_r.at[0, dx, 2])
        return value + ra1[0, dx].astype(f32) + ra1[1, dx].astype(f32)

    def summed_b(dy):
        value = pb[dy, 0].astype(f32)
        all_arrived(rb1.at[0:2, dy], g1_r.at[1, dy, 2])
        return value + rb1[0, dy].astype(f32) + rb1[1, dy].astype(f32)

    def second(axis, position, count, k, source, target, which):
        copy = pltpu.make_async_remote_copy(
            src_ref=source.at[k - 1], dst_ref=target.at[k - 1],
            send_sem=g_s.at[which], recv_sem=g_r.at[which],
            device_id={axis: lax.rem(position + k, count)}, device_id_type=ID,
        )
        copy.start()

    left += [(sa2, g_s.at[0]), (sb2, g_s.at[1])]

    def second_both(k):
        sa2[k - 1] = summed_a(k).astype(bf16)
        second("seq_1", xx, nx, k, sa2, ra2, 0)
        sb2[k - 1] = summed_b(k).astype(bf16)
        second("seq_0", yy, ny, k, sb2, rb2, 1)

    pass_both(1)
    second_both(2)
    pass_both(3)
    second_both(1)
    pass_both(0)
    second_both(3)

    def key_body(b, i, at, cols):
        grad_key = gkp[b, i] + dot(v[at, cols], following[b, i], NT)
        gk_ref[at, cols] = grad_key.astype(bf16)

    each_block(key_body)

    final_a, final_b = summed_a(0), summed_b(0)

    def last(final, received, which):
        all_arrived(received, g_r.at[which])
        for kk in range(received.shape[0]):
            final += received[kk].astype(f32)
        final = final.T
        tzf[which] = final
        tz[which] = final.astype(bf16)
        left.append((tz.at[which, 0 : (nz - 1) * rows], g_s.at[2 + which]))
        exchange(
            "seq_2", nz, lambda p: tz.at[which, pl.ds(pl.multiple_of(p * rows, rows), rows)],
            lambda kk: rz.at[which, kk - 1], g_s.at[2 + which], g_r.at[2 + which], True,
        )

    last(final_a, ra2, 0)
    last(final_b, rb2, 1)
    for which in range(2):
        result = tzf[which, pl.ds(pl.multiple_of(zh * rows, rows), rows)]
        all_arrived(rz.at[which], g_r.at[2 + which])
        for kk in range(nz - 1):
            result += rz[which, kk].astype(f32)
        gl_ref[:, which * side : (which + 1) * side] = result

    for copy in sent:
        copy.wait_send()

    for ref, semaphore in left:
        all_left(ref, semaphore)

    @pl.loop(0, nl)
    def _(block):
        place = xg.at[block, cc]
        all_left(place, xs_s.at[block])
        ahead = jnp.logical_and(zl == nl - 2, block == 0)
        behind = jnp.logical_and(zl == 1, block == nl - 1)

        @pl.when(jnp.logical_and(jnp.logical_and(block <= zl, zl < nl - 1), jnp.logical_not(ahead)))
        def _():
            all_left(place, xp_s.at[block])

        @pl.when(jnp.logical_and(jnp.logical_and(block >= zl, zl > 0), jnp.logical_not(behind)))
        def _():
            all_left(place, xm_s.at[block])


def deliver(*refs):
    copies = [pltpu.make_async_copy(refs[i], refs[4 + i], refs[8].at[i]) for i in range(4)]
    for copy in copies:
        copy.start()
    for copy in copies:
        copy.wait()


def per_device(inputs, latent, queries, keys, grad_out):
    sizes = tuple(lax.axis_size(a) for a in (*SEQ, "head_0"))
    ny, nx, nz, nl = sizes
    tokens, feats = inputs.shape
    rows, columns = latent.shape
    heads, blocks = columns // DK, tokens // BLOCK
    seqs, everyone = ny * nx * nz, ny * nx * nz * rows
    side, piece = columns // 2, nz * rows
    dma = pltpu.SemaphoreType.DMA
    most = max(ny, nx, nz) - 1
    scratch = [
        pltpu.VMEM(latent.shape, f32),
        pltpu.VMEM((tokens, columns), bf16),
        pltpu.VMEM((tokens, columns), bf16),
        pltpu.VMEM((tokens, columns), bf16),
        pltpu.VMEM((seqs, rows // 2, columns), bf16),
        pltpu.VMEM((seqs, rows // 2, columns), bf16),
        pltpu.VMEM((everyone, columns), bf16),
        pltpu.VMEM((nl, 2, tokens, feats), bf16),
        pltpu.VMEM((tokens, columns), f32),
        pltpu.VMEM((tokens, columns), bf16),
        pltpu.VMEM((blocks, heads, BLOCK, BLOCK), bf16),
        pltpu.VMEM((blocks, heads, DK, DK), f32),
        pltpu.VMEM((blocks, heads, DK, DK), bf16),
        pltpu.VMEM((blocks, heads, BLOCK, DK), f32),
        pltpu.VMEM((tokens, columns), bf16),
        pltpu.VMEM((blocks, heads, DK, DK), f32),
        pltpu.VMEM((blocks, heads, DK, DK), bf16),
        pltpu.VMEM((blocks, heads, BLOCK, DK), f32),
        pltpu.VMEM((blocks, heads, BLOCK, DK), f32),
        pltpu.VMEM((columns, tokens), bf16),
        pltpu.VMEM((heads, DK, DK), f32),
        pltpu.VMEM((2, heads, PIECES, 4, DK // PIECES, DK), bf16),
        pltpu.VMEM((2, heads, PIECES, 2, most, DK // PIECES, DK), bf16),
        pltpu.VMEM((2, heads, PIECES, 3, DK // PIECES, DK), bf16),
        pltpu.VMEM((heads, DK, DK), f32),
        pltpu.VMEM((ny, nx, side, piece), bf16),
        pltpu.VMEM((ny, nx, side, piece), bf16),
        pltpu.VMEM((ny - 1, nx, side, piece), bf16),
        pltpu.VMEM((nx - 1, ny, side, piece), bf16),
        pltpu.VMEM((nx - 1, side, piece), bf16),
        pltpu.VMEM((ny - 1, side, piece), bf16),
        pltpu.VMEM((nx - 1, side, piece), bf16),
        pltpu.VMEM((ny - 1, side, piece), bf16),
        pltpu.VMEM((2, piece, side), bf16),
        pltpu.VMEM((2, piece, side), f32),
        pltpu.VMEM((2, nz - 1, rows, side), bf16),
        dma((5,)),
        dma((6,)), dma((6,)),
        dma((2,)), dma((2,)),
        dma((2,)), dma((2,)),
        dma((nl,)), dma((nl,)), dma((nl,)),
        dma((nl, CHUNKS)), dma((nl, CHUNKS)),
        dma((2, heads, PIECES, 2)), dma((2, heads, PIECES, 2)),
        dma((2, heads, PIECES)), dma((2, heads, PIECES)),
        dma((2, 4)), dma((2, 4, 3)),
        dma((4,)), dma((4,)),
    ]
    like = jax.ShapeDtypeStruct(queries.shape, bf16)
    results = pl.pallas_call(
        functools.partial(kernel, sizes),
        out_shape=(like, like, like, jax.ShapeDtypeStruct(latent.shape, f32)),
        in_specs=[pl.BlockSpec(memory_space=pltpu.HBM)] * 5,
        out_specs=(pl.BlockSpec(memory_space=pltpu.VMEM),) * 4,
        scratch_shapes=scratch,
        compiler_params=pltpu.CompilerParams(
            collective_id=0, has_side_effects=True, vmem_limit_bytes=40 << 20
        ),
    )(*(pltpu.with_memory_space_constraint(a, pltpu.HBM) for a in (inputs, latent, queries, keys, grad_out)))
    return pl.pallas_call(
        deliver,
        out_shape=(like, like, like, jax.ShapeDtypeStruct(latent.shape, f32)),
        in_specs=[pl.BlockSpec(memory_space=pltpu.VMEM)] * 4,
        out_specs=(pl.BlockSpec(memory_space=pltpu.HBM),) * 4,
        scratch_shapes=[pltpu.SemaphoreType.DMA((4,))],
        compiler_params=pltpu.CompilerParams(vmem_limit_bytes=4 << 20),
    )(*results)


def solution(mesh):
    torus = Mesh(mesh.devices.reshape(4, 4, 4, 4, 2), (*SEQ, *HEAD))
    placed = P(SEQ, HEAD)
    return jax.shard_map(
        per_device,
        mesh=torus,
        in_specs=(placed,) * 5,
        out_specs=(placed,) * 4,
        check_vma=False,
    )
```
